32 devices in a mesh: gx: 8 (over y, x, core), gy: 4 (over z).
Axes of the slice: x: 2, y: 2, z: 4, core: 2. Of those that a mesh axis runs over, the one named last changes fastest.
Arguments:
- load_cases: float32 [16, 12, 64, 128], P('gx', 'gy')
- matrix_tiles: float32 [16, 12, 64, 320], P('gx', 'gy')
- block_cols: int32 [16, 12, 5], P('gx', 'gy'), may hold values from 1 to 18, as said below
- smoother_blocks: float32 [16, 12, 4096], P('gx', 'gy')
- near_null: float32 [16, 12, 384], P('gx', 'gy'), may hold values from -0.75 to 0.75
- coarse_map: int32 [16, 12], P('gx', 'gy'), may hold values from 0 to 31, as said below
- coarse_inverse: float32 [192, 192], P(('gx', 'gy')), as said below
Outputs:
- solution: float32 [16, 12, 64, 128], P('gx', 'gy')
- residual: float32 [16, 12, 64, 128], P('gx', 'gy')
The draws below stay inside these ranges and needn't reach their ends.
Inputs may be any that keep to these rules, and one draw needn't show every extreme that they name: `block_cols`: each aggregate's 5 slots name the aggregate itself and its four grid neighbours, each once, in an order drawn for each aggregate, as row-major indices (row width 3 + 2) into the device's block of aggregates extended by one aggregate on every side. `coarse_map`: all aggregates of one device's block of 2 x 3 aggregates map to one coarse aggregate, and different blocks to different coarse aggregates. coarse_inverse is symmetric.
All inputs are finite; a program needn't handle non-finite values.
Results may differ from the reference program's by a relative error of at most 0.0003.
Values sent between devices are 32-bit elements; how exact they have to be, the bound alone decides.
A program may use at most 64 MiB of HBM per device.

```python
import math
import jax
import jax.numpy as jnp
from jax import lax

AX = 2
AY = 3
BLK = 64
SLOTS = 5
NULLS = 6
R = 128
NAX = 16
NAY = 12
NCA = 32
NC = 192


def slot_order(key):
    scores = jax.random.randint(jax.random.fold_in(key, 17), (NAX, NAY, SLOTS), 0, 1 << 20) * 8
    scores = scores + jnp.arange(SLOTS, dtype=jnp.int32)[None, None, :]
    return jnp.argsort(scores, axis=-1).astype(jnp.int32)


def draw_block_cols(key, part):
    order = slot_order(key)
    row_steps = jnp.array([0, -1, 1, 0, 0], dtype=jnp.int32)[order]
    col_steps = jnp.array([0, 0, 0, -1, 1], dtype=jnp.int32)[order]
    local_rows = (jnp.arange(NAX, dtype=jnp.int32) % AX)[:, None, None]
    local_cols = (jnp.arange(NAY, dtype=jnp.int32) % AY)[None, :, None]
    return ((local_rows + 1 + row_steps) * (AY + 2) + local_cols + 1 + col_steps).astype(jnp.int32)


def draw_coarse_map(key, part):
    shuffled = jax.random.permutation(jax.random.fold_in(key, 61), NCA).astype(jnp.int32)
    block_rows = (jnp.arange(NAX, dtype=jnp.int32) // AX)[:, None]
    block_cols_here = (jnp.arange(NAY, dtype=jnp.int32) // AY)[None, :]
    owner = (block_rows * (NAY // AY) + block_cols_here).astype(jnp.int32)
    return shuffled[owner].astype(jnp.int32)


def draw_matrix_tiles(key, part):
    order = slot_order(key)
    self_slot = (order == 0).astype(jnp.float32)[:, :, None, :, None]
    noise = jax.random.uniform(jax.random.fold_in(key, 29), (NAX, NAY, BLK, SLOTS, BLK), jnp.float32, -1.0, 1.0)
    amplitude = self_slot * (0.025 / BLK) + (1.0 - self_slot) * (0.75 / (4.0 * BLK))
    identity = (jnp.arange(BLK)[:, None] == jnp.arange(BLK)[None, :]).astype(jnp.float32)
    diagonal = self_slot * identity[None, None, :, None, :]
    return (noise * amplitude + diagonal).reshape(NAX, NAY, BLK, SLOTS * BLK)


def draw_smoother_blocks(key, part):
    noise = jax.random.uniform(jax.random.fold_in(key, 41), (NAX, NAY, BLK, BLK), jnp.float32, -1.0, 1.0)
    identity = (jnp.arange(BLK)[:, None] == jnp.arange(BLK)[None, :]).astype(jnp.float32)
    blocks = 0.9 * identity[None, None, :, :] + noise * (0.8 / BLK)
    return blocks.reshape(NAX, NAY, BLK * BLK)


def draw_load_cases(key, part):
    sample = jnp.clip(jax.random.normal(jax.random.fold_in(key, 3), (NAX, NAY, BLK, R), jnp.float32), -6.0, 6.0)
    row_scale = jnp.exp(jax.random.uniform(jax.random.fold_in(key, 5), (NAX, NAY), jnp.float32, math.log(0.3), math.log(3.0)))
    case_scale = jnp.exp(jax.random.uniform(jax.random.fold_in(key, 6), (R,), jnp.float32, math.log(0.3), math.log(3.0)))
    grid_rows = jnp.arange(NAX, dtype=jnp.float32) / (NAX - 1)
    grid_cols = jnp.arange(NAY, dtype=jnp.float32) / (NAY - 1)
    rising = 0.6 + 0.6 * (grid_rows[:, None] + grid_cols[None, :])
    return sample * (row_scale * rising)[:, :, None, None] * case_scale[None, None, None, :]


def draw_coarse_inverse(key, part):
    sample = jnp.clip(jax.random.normal(jax.random.fold_in(key, 53), (NC, NC), jnp.float32), -6.0, 6.0)
    identity = (jnp.arange(NC)[:, None] == jnp.arange(NC)[None, :]).astype(jnp.float32)
    return (sample + sample.T) * (0.3 * (2.0 * NC) ** (-0.5)) + 0.8 * identity


def levels(stream_key, extent, cuts, low, high):
    factor_of = 1.0
    for dim, blocks in cuts:
        draws = jax.random.uniform(jax.random.fold_in(jax.random.fold_in(stream_key, 6), dim), (blocks,), jnp.float32, low / len(cuts), high / len(cuts))
        factor_of = factor_of * jnp.repeat(jnp.exp(draws), extent[dim] // blocks).reshape((-1,) + (1,) * (len(extent) - 1 - dim))
    return factor_of


def scatter_about(own_key, extent, deviation, limit, shards=(), held_as=jnp.bfloat16):
    entries = jax.random.normal(own_key, extent, jnp.float32) * deviation
    if len(shards) > 0:
        entries = levels(own_key, extent, shards, -0.22, 0.18) * entries
    return jnp.clip(entries, min=-limit, max=limit).astype(held_as)


def setup_inputs(seed: int = 0) -> dict:
    keys = jax.random.split(jax.random.key(seed), 8)
    return {
        "load_cases": draw_load_cases(jax.random.fold_in(keys[7], 71), 0),
        "matrix_tiles": draw_matrix_tiles(jax.random.fold_in(keys[7], 71), 0),
        "block_cols": draw_block_cols(jax.random.fold_in(keys[7], 71), 0),
        "smoother_blocks": draw_smoother_blocks(jax.random.fold_in(keys[7], 71), 0),
        "near_null": scatter_about(keys[4], (NAX, NAY, NULLS * BLK), BLK ** -0.5, 0.75, ((0, 8), (1, 4)), jnp.float32),
        "coarse_map": draw_coarse_map(jax.random.fold_in(keys[7], 71), 0),
        "coarse_inverse": draw_coarse_inverse(jax.random.fold_in(keys[7], 71), 0),
    }


relax_weight = 0.8
highest = lax.Precision.HIGHEST


def apply_operator(vector_field, matrix_tiles, block_cols):
    padded = jnp.pad(vector_field, ((1, 1), (1, 1), (0, 0), (0, 0)))
    grid_rows = jnp.arange(NAX, dtype=jnp.int32)
    grid_cols = jnp.arange(NAY, dtype=jnp.int32)
    row_first = (grid_rows - grid_rows % AX)[:, None, None]
    col_first = (grid_cols - grid_cols % AY)[None, :, None]
    source_rows = (row_first + block_cols // (AY + 2)).astype(jnp.int32)
    source_cols = (col_first + block_cols % (AY + 2)).astype(jnp.int32)

    def one_row(inputs):
        tile_row, rows_here, cols_here = inputs
        picked = padded[rows_here, cols_here].reshape(NAY, SLOTS * BLK, R)
        return jnp.einsum("jbk,jkr->jbr", tile_row, picked, precision=highest)

    return lax.map(one_row, (matrix_tiles, source_rows, source_cols))


def relax(defect, smoother_blocks):
    blocks = smoother_blocks.reshape(NAX, NAY, BLK, BLK)
    return relax_weight * jnp.einsum("ijab,ijbr->ijar", blocks, defect, precision=highest)


def coarse_correct(defect, near_null, coarse_map, coarse_inverse):
    modes = near_null.reshape(NAX, NAY, NULLS, BLK)
    onehot = (coarse_map[:, :, None] == jnp.arange(NCA, dtype=jnp.int32)[None, None, :]).astype(jnp.float32)
    contrib = jnp.einsum("ijkb,ijbr->ijkr", modes, defect, precision=highest)
    gathered = jnp.einsum("ijc,ijkr->ckr", onehot, contrib, precision=highest).reshape(NC, R)
    values = jnp.dot(coarse_inverse, gathered, precision=highest)
    coarse_back = jnp.einsum("ijc,ckr->ijkr", onehot, values.reshape(NCA, NULLS, R), precision=highest)
    return jnp.einsum("ijkb,ijkr->ijbr", modes, coarse_back, precision=highest)


def reference(load_cases, matrix_tiles, block_cols, smoother_blocks, near_null, coarse_map, coarse_inverse):
    def operate(vector_field):
        return apply_operator(vector_field, matrix_tiles, block_cols)

    def smooth(defect):
        return relax(defect, smoother_blocks)

    def correct(defect):
        return coarse_correct(defect, near_null, coarse_map, coarse_inverse)

    first = smooth(load_cases)
    first = first + correct(load_cases - operate(first))
    precond = first + smooth(load_cases - operate(first))
    defect = load_cases - operate(precond)
    update = smooth(defect)
    update = update + correct(defect - operate(update))
    update = update + smooth(defect - operate(update))
    precond = precond + update
    image = operate(precond)
    aligned = jnp.sum(load_cases * precond, axis=(0, 1, 2))
    curved = jnp.sum(precond * image, axis=(0, 1, 2))
    alpha = aligned / curved
    solution = alpha * precond
    residual = load_cases - alpha * image
    return (solution, residual)
```

```python
import functools

import jax
import jax.numpy as jnp
from jax import lax
from jax.experimental import pallas as pl
from jax.experimental.pallas import tpu as pltpu
from jax.sharding import PartitionSpec as P

relax_weight = 0.8
highest = lax.Precision.HIGHEST


def padded(cells, sides, width):
    for axis, dim in sides:
        count = lax.axis_size(axis)
        ends = count - 1
        head = lax.slice_in_dim(cells, 0, width, axis=dim)
        tail = lax.slice_in_dim(cells, cells.shape[dim] - width, cells.shape[dim], axis=dim)
        cells = jnp.concatenate(
            [
                lax.ppermute(tail, axis, [(i, (i + 1) % count) for i in range(ends)]),
                cells,
                lax.ppermute(head, axis, [((i + 1) % count, i) for i in range(ends)]),
            ],
            axis=dim,
        )
    return cells


def cut(v):
    hi = v.astype(jnp.bfloat16)
    return hi, (v - hi.astype(jnp.float32)).astype(jnp.bfloat16)


def stacked(v):
    hi, lo = cut(v)
    return jnp.concatenate([hi, lo, hi], axis=0)


def mm(a, b):
    return lax.dot_general(a, b, (((1,), (0,)), ((), ())), preferred_element_type=jnp.float32)


def mm_t(a, b, precision=None):
    return lax.dot_general(
        a, b, (((1,), (1,)), ((), ())), precision=precision, preferred_element_type=jnp.float32
    )


def mm3(a_cut, b):
    hi, lo = cut(b)
    return mm(a_cut[0], hi) + (mm(a_cut[0], lo) + mm(a_cut[1], hi))


def step_kernel(
    nx, ny, modes,
    b_ref, a_ref, cols_ref, s_ref, n_ref, map_ref, inv_ref,
    sol_ref, res_ref,
    field, up, down, left, right, local, edge, smoother, info, info_all, near, coarse, coarse_all,
    sums, sums_all, halo_send, halo_recv, near_send, near_recv, all_send, all_recv,
):
    rows, cols, blk, cases = b_ref.shape
    count = rows * cols
    size = count * blk
    n = nx * ny
    width = info.shape[1]
    coarse_rows = n * 8
    x, y = lax.axis_index("gx"), lax.axis_index("gy")
    me = x * ny + y
    sides = (
        (x > 0, (x - 1, y)),
        (x < nx - 1, (x + 1, y)),
        (y > 0, (x, y - 1)),
        (y < ny - 1, (x, y + 1)),
    )
    halos = (up, down, left, right)

    barrier = pltpu.get_barrier_semaphore()

    def greet(j, carry):
        peer = lax.rem(me + j, n)
        pl.semaphore_signal(
            barrier, inc=1, device_id=(peer // ny, lax.rem(peer, ny)),
            device_id_type=pl.DeviceIdType.MESH,
        )
        return carry

    lax.fori_loop(1, n, greet, 0)

    def send_all(src, dst, k):
        def one(j, carry):
            peer = lax.rem(me + j, n)
            pltpu.make_async_remote_copy(
                src_ref=src, dst_ref=dst.at[me],
                send_sem=all_send.at[k], recv_sem=all_recv.at[k],
                device_id=(peer // ny, lax.rem(peer, ny)),
                device_id_type=pl.DeviceIdType.MESH,
            ).start()
            return carry

        lax.fori_loop(1, n, one, 0)

    def wait_all(dst, sem):
        others = dst.at[pl.ds(0, n - 1)]
        pltpu.make_async_copy(others, others, sem).wait()

    def halo_copies(k):
        now = field.at[k]
        out = (
            (now.at[0], down.at[k], 1),
            (now.at[rows - 1], up.at[k], 0),
            (now.at[:, 0], right.at[k], 3),
            (now.at[:, cols - 1], left.at[k], 2),
        )
        return [
            pltpu.make_async_remote_copy(
                src_ref=src, dst_ref=dst,
                send_sem=halo_send.at[k, side], recv_sem=halo_recv.at[k, lands],
                device_id=peer, device_id_type=pl.DeviceIdType.MESH,
            )
            for side, ((src, dst, lands), (_, peer)) in enumerate(zip(out, sides))
        ]

    def halo_start(k):
        for (here, _), copy in zip(sides, halo_copies(k)):
            pl.when(here)(copy.start)

    def halo_wait(k):
        for side, (here, _) in enumerate(sides):
            buf = halos[side].at[k]
            pl.when(here)(pltpu.make_async_copy(buf, buf, halo_recv.at[k, side]).wait)

    def near_copies():
        return [
            pltpu.make_async_remote_copy(
                src_ref=n_ref, dst_ref=near.at[lands],
                send_sem=near_send.at[side], recv_sem=near_recv.at[lands],
                device_id=peer, device_id_type=pl.DeviceIdType.MESH,
            )
            for side, (lands, (_, peer)) in enumerate(zip((1, 0, 3, 2), sides))
        ]

    for p in range(count):
        hi, lo = cut(relax_weight * s_ref[p])
        smoother[p] = jnp.concatenate([hi, hi, lo], axis=1)

    def smooth(v):
        return jnp.concatenate(
            [mm(smoother[p], stacked(v[p * blk : (p + 1) * blk])) for p in range(count)], axis=0
        )

    b = b_ref[...].reshape(size, cases)
    first = smooth(b)
    field[0] = first.reshape(rows, cols, blk, cases)
    for side, (here, _) in enumerate(sides):

        @pl.when(jnp.logical_not(here))
        def _():
            halos[side][...] = jnp.zeros_like(halos[side])
            near[side] = jnp.zeros_like(near[side])

    info[...] = jnp.zeros_like(info)
    info[0:modes, 0 : inv_ref.shape[1]] = inv_ref[...]
    info[modes : modes + 1, :] = jnp.full((1, width), map_ref[0, 0].astype(jnp.float32))

    pl.semaphore_wait(barrier, n - 1)
    halo_start(0)
    for (here, _), copy in zip(sides, near_copies()):
        pl.when(here)(copy.start)
    send_all(info, info_all, 0)
    info_all[pl.ds(me, 1)] = info[...][None]

    local[...] = jnp.zeros_like(local)
    for i in range(rows):
        for j in range(cols):
            p = i * cols + j
            tiles = [a_ref[i, j, :, s * blk : (s + 1) * blk] for s in range(5)]
            names = [cols_ref[i, j, s] for s in range(5)]
            for d, (di, dj) in enumerate(((0, 0), (-1, 0), (1, 0), (0, -1), (0, 1))):
                e = (i + 1 + di) * (cols + 2) + j + 1 + dj
                tile = tiles[0] * (names[0] == e).astype(jnp.float32)
                for s in range(1, 5):
                    tile = tile + tiles[s] * (names[s] == e).astype(jnp.float32)
                hi, lo = cut(tile)
                ii, jj = i + di, j + dj
                if 0 <= ii < rows and 0 <= jj < cols:
                    q = ii * cols + jj
                    for k, part in enumerate((hi, hi, lo)):
                        at = k * size + q * blk
                        local[p * blk : (p + 1) * blk, at : at + blk] = part
                else:
                    at = (0, j, cols + j, 2 * cols + i, 2 * cols + rows + i)[d]
                    edge[at] = jnp.concatenate([hi, hi, lo], axis=1)

    def places():
        for j in range(cols):
            yield 0, j, j, j
        for j in range(cols):
            yield 1, j, cols + j, (rows - 1) * cols + j
        for i in range(rows):
            yield 2, i, 2 * cols + i, i * cols
        for i in range(rows):
            yield 3, i, 2 * cols + rows + i, i * cols + cols - 1

    def operate(v, k):
        inner = mm(local[...], stacked(v))
        parts = [inner[p * blk : (p + 1) * blk] for p in range(count)]
        halo_wait(k)
        for side, at, e, p in places():
            parts[p] = parts[p] + mm(edge[e], stacked(halos[side][k, at]))
        return jnp.concatenate(parts, axis=0)

    own_n = n_ref[...]
    own_hi, own_lo = cut(own_n)
    own_cat = jnp.concatenate([own_hi, own_hi, own_lo], axis=1)

    def restrict(v, k):
        g = mm(own_cat, stacked(v))
        coarse[k] = g
        send_all(coarse.at[k], coarse_all.at[k], 1 + k)
        coarse_all[k, pl.ds(me, 1)] = g[None]

    r = b - operate(first, 0)
    restrict(r, 0)

    for side, (here, _) in enumerate(sides):
        buf = near.at[side]
        pl.when(here)(pltpu.make_async_copy(buf, buf, near_recv.at[side]).wait)

    def at_rows(t, v):
        pieces = [jnp.zeros_like(v)] * 6
        pieces[t] = v
        return jnp.concatenate(pieces, axis=0)

    def across(v):
        hi, lo = cut(v)
        return jnp.concatenate([hi, lo, hi], axis=1)

    spread = mm_t(local[...], across(at_rows(0, own_n)))
    parts = [spread[p * blk : (p + 1) * blk] for p in range(count)]
    theirs = [near[side] for side in range(4)]
    facing = (
        lambda at: (rows - 1) * cols + at,
        lambda at: at,
        lambda at: at * cols + cols - 1,
        lambda at: at * cols,
    )
    for side, at, e, p in places():
        q = facing[side](at)
        block = theirs[side][:, q * blk : (q + 1) * blk]
        parts[p] = parts[p] + mm_t(edge[e], across(at_rows(1 + side, block)))
    spread_cut = cut(jnp.concatenate(parts, axis=0))
    eye = (
        lax.broadcasted_iota(jnp.int32, (size, size), 0)
        == lax.broadcasted_iota(jnp.int32, (size, size), 1)
    ).astype(jnp.float32).astype(jnp.bfloat16)
    prolong_cut = tuple(
        mm_t(eye, part).astype(jnp.bfloat16) for part in cut(at_rows(0, own_n))
    )

    wait_all(info_all, all_recv.at[0])
    inv_all = info_all[...].reshape(coarse_rows, width)
    ids = [me] + [
        jnp.clip(px, 0, nx - 1) * ny + jnp.clip(py, 0, ny - 1) for _, (px, py) in sides
    ]
    lane = lax.broadcasted_iota(jnp.int32, (8, coarse_rows), 1)
    row = lax.broadcasted_iota(jnp.int32, (8, coarse_rows), 0)
    pick = []
    for d in ids:
        tile = info_all[pl.ds(d, 1)].reshape(8, width)
        label = jnp.broadcast_to(tile[modes : modes + 1, 0:1], (8, coarse_rows))
        wanted = label * 8.0 + row.astype(jnp.float32)
        hit = jnp.where(lane.astype(jnp.float32) == wanted, 1.0, 0.0)
        pick.append(jnp.where(row < modes, hit, 0.0))
    pick.append(jnp.zeros((8, coarse_rows), jnp.float32))
    picked = lax.dot_general(
        jnp.concatenate(pick, axis=0), inv_all, (((1,), (0,)), ((), ())),
        precision=highest, preferred_element_type=jnp.float32,
    )
    lane3 = lax.broadcasted_iota(jnp.int32, (n, 8, width), 2).astype(jnp.float32)
    row3 = lax.broadcasted_iota(jnp.int32, (n, 8, width), 1)
    labels = jnp.broadcast_to(info_all[...][:, modes : modes + 1, :], (n, 8, width))
    order = jnp.where(lane3 == labels * float(modes) + row3.astype(jnp.float32), 1.0, 0.0)
    order = jnp.where(row3 < modes, order, 0.0).reshape(coarse_rows, width)
    solve_cut = cut(mm_t(picked, order, precision=highest))

    def correct(k):
        wait_all(coarse_all.at[k], all_recv.at[1 + k])
        h = mm3(solve_cut, coarse_all[k].reshape(coarse_rows, cases))
        return mm3(prolong_cut, h), mm3(spread_cut, h)

    def relax(v, k):
        s = smooth(v)
        field[k] = s.reshape(rows, cols, blk, cases)
        halo_start(k)
        return s, v - operate(s, k)

    up_by, down_by = correct(0)
    precond = first + up_by
    r = r - down_by
    s, r = relax(r, 1)
    precond = precond + s
    s, r = relax(r, 2)
    precond = precond + s
    restrict(r, 1)
    up_by, down_by = correct(1)
    precond = precond + up_by
    r = r - down_by
    s, r = relax(r, 3)
    precond = precond + s

    image = b - r
    sums[...] = jnp.concatenate(
        [
            jnp.sum(b * precond, axis=0, keepdims=True),
            jnp.sum(precond * image, axis=0, keepdims=True),
            jnp.zeros((6, cases), jnp.float32),
        ],
        axis=0,
    )
    send_all(sums, sums_all, 3)
    sums_all[pl.ds(me, 1)] = sums[...][None]
    wait_all(sums_all, all_recv.at[3])
    total = jnp.sum(sums_all[...], axis=0)
    alpha = total[0:1] / total[1:2]
    sol_ref[...] = (alpha * precond).reshape(rows, cols, blk, cases)
    res_ref[...] = (b - alpha * image).reshape(rows, cols, blk, cases)

    for k in range(4):
        for (here, _), copy in zip(sides, halo_copies(k)):
            pl.when(here)(copy.wait_send)
    for (here, _), copy in zip(sides, near_copies()):
        pl.when(here)(copy.wait_send)
    wait_all(info_all, all_send.at[0])
    wait_all(coarse_all.at[0], all_send.at[1])
    wait_all(coarse_all.at[1], all_send.at[2])
    wait_all(sums_all, all_send.at[3])


def fused(
    nx, ny,
    load_cases, matrix_tiles, block_cols, smoother_blocks, near_null, coarse_map, coarse_inverse
):
    rows, cols, blk, cases = load_cases.shape
    count = rows * cols
    modes = near_null.shape[2] // blk
    n = nx * ny
    width = -(-coarse_inverse.shape[1] // 128) * 128
    near = jnp.transpose(near_null.reshape(count, modes, blk), (1, 0, 2)).reshape(modes, -1)
    near = jnp.pad(near, ((0, 8 - modes), (0, 0)))
    blocks = smoother_blocks.reshape(count, blk, blk)
    vmem = pl.BlockSpec(memory_space=pltpu.VMEM)
    smem = pl.BlockSpec(memory_space=pltpu.SMEM)
    f32, bf16 = jnp.float32, jnp.bfloat16
    shape = jax.ShapeDtypeStruct(load_cases.shape, f32)
    return pl.pallas_call(
        functools.partial(step_kernel, nx, ny, modes),
        out_shape=(shape, shape),
        in_specs=[vmem, vmem, smem, vmem, vmem, smem, vmem],
        out_specs=(vmem, vmem),
        scratch_shapes=[
            pltpu.VMEM((4, rows, cols, blk, cases), f32),
            pltpu.VMEM((4, cols, blk, cases), f32),
            pltpu.VMEM((4, cols, blk, cases), f32),
            pltpu.VMEM((4, rows, blk, cases), f32),
            pltpu.VMEM((4, rows, blk, cases), f32),
            pltpu.VMEM((count * blk, 3 * count * blk), bf16),
            pltpu.VMEM((2 * (rows + cols), blk, 3 * blk), bf16),
            pltpu.VMEM((count, blk, 3 * blk), bf16),
            pltpu.VMEM((8, width), f32),
            pltpu.VMEM((n, 8, width), f32),
            pltpu.VMEM((4, 8, count * blk), f32),
            pltpu.VMEM((2, 8, cases), f32),
            pltpu.VMEM((2, n, 8, cases), f32),
            pltpu.VMEM((8, cases), f32),
            pltpu.VMEM((n, 8, cases), f32),
            pltpu.SemaphoreType.DMA((4, 4)),
            pltpu.SemaphoreType.DMA((4, 4)),
            pltpu.SemaphoreType.DMA((4,)),
            pltpu.SemaphoreType.DMA((4,)),
            pltpu.SemaphoreType.DMA((4,)),
            pltpu.SemaphoreType.DMA((4,)),
        ],
        compiler_params=pltpu.CompilerParams(
            collective_id=0, has_side_effects=True, vmem_limit_bytes=60 * 2**20
        ),
    )(load_cases, matrix_tiles, block_cols, blocks, near, coarse_map, coarse_inverse)


def per_device(
    load_cases, matrix_tiles, block_cols, smoother_blocks, near_null, coarse_map, coarse_inverse
):
    agg_rows, agg_cols, block_size, case_count = load_cases.shape
    mode_count = near_null.shape[2] // block_size
    coarse_total = coarse_inverse.shape[1]
    coarse_aggs = coarse_total // mode_count
    modes = near_null.reshape(agg_rows, agg_cols, mode_count, block_size)
    inverse_blocks = smoother_blocks.reshape(agg_rows, agg_cols, block_size, block_size)

    def operate(vector_field):
        extended = padded(vector_field, (("gx", 0), ("gy", 1)), 1)
        flattened = extended.reshape(-1, block_size, case_count)
        picked = flattened[block_cols].reshape(agg_rows, agg_cols, -1, case_count)
        return jnp.einsum("ijbk,ijkr->ijbr", matrix_tiles, picked, precision=highest)

    def smooth(defect):
        return relax_weight * jnp.einsum(
            "ijab,ijbr->ijar", inverse_blocks, defect, precision=highest
        )

    def correct(defect):
        contrib = jnp.einsum("ijkb,ijbr->ijkr", modes, defect, precision=highest)
        own_part = jnp.sum(contrib, axis=(0, 1))
        my_label = coarse_map[0, 0]
        label_value = jnp.reshape(my_label.astype(jnp.float32), (1,))
        pieces, labels = (
            lax.all_gather(own_part[None], ("gx", "gy"), axis=0, tiled=True),
            lax.all_gather(label_value, ("gx", "gy"), axis=0, tiled=True),
        )
        label_ids = labels.astype(jnp.int32)
        placing = (label_ids[:, None] == jnp.arange(coarse_aggs, dtype=jnp.int32)[None, :]).astype(
            jnp.float32
        )
        ordered = jnp.einsum("dc,dkr->ckr", placing, pieces, precision=highest).reshape(
            coarse_total, case_count
        )
        own_rows = jnp.dot(coarse_inverse, ordered, precision=highest)
        solved = lax.all_gather(own_rows, ("gx", "gy"), axis=0, tiled=True)
        mine = lax.dynamic_slice_in_dim(solved, my_label * mode_count, mode_count, 0)
        coarse_back = jnp.broadcast_to(
            mine[None, None], (agg_rows, agg_cols, mode_count, case_count)
        )
        return jnp.einsum("ijkb,ijkr->ijbr", modes, coarse_back, precision=highest)

    first = smooth(load_cases)
    first = first + correct(load_cases - operate(first))
    precond = first + smooth(load_cases - operate(first))
    defect = load_cases - operate(precond)
    update = smooth(defect)
    update = update + correct(defect - operate(update))
    update = update + smooth(defect - operate(update))
    precond = precond + update
    local_aligned = jnp.sum(load_cases * precond, axis=(0, 1, 2))
    aligned = lax.psum(local_aligned, ("gx", "gy"))
    image = operate(precond)
    curved = lax.psum(jnp.sum(precond * image, axis=(0, 1, 2)), ("gx", "gy"))
    alpha = aligned / curved
    solution = alpha * precond
    residual = load_cases - alpha * image
    return (solution, residual)


def solution(mesh):
    nx, ny = mesh.shape["gx"], mesh.shape["gy"]
    step = functools.partial(fused, nx, ny) if nx * ny <= 128 else per_device
    placed = (
        P("gx", "gy", None, None),
        P("gx", "gy", None, None),
        P("gx", "gy", None),
        P("gx", "gy", None),
        P("gx", "gy", None),
        P("gx", "gy"),
        P(("gx", "gy"), None),
    )
    return jax.shard_map(
        step,
        mesh=mesh,
        in_specs=placed,
        out_specs=(P("gx", "gy", None, None), P("gx", "gy", None, None)),
        check_vma=False,
    )
```

```python
import functools

import jax
import jax.numpy as jnp
from jax import lax
from jax.experimental import pallas as pl
from jax.experimental.pallas import tpu as pltpu
from jax.sharding import PartitionSpec as P

relax_weight = 0.8
highest = lax.Precision.HIGHEST


def padded(cells, sides, width):
    for axis, dim in sides:
        count = lax.axis_size(axis)
        ends = count - 1
        head = lax.slice_in_dim(cells, 0, width, axis=dim)
        tail = lax.slice_in_dim(cells, cells.shape[dim] - width, cells.shape[dim], axis=dim)
        cells = jnp.concatenate(
            [
                lax.ppermute(tail, axis, [(i, (i + 1) % count) for i in range(ends)]),
                cells,
                lax.ppermute(head, axis, [((i + 1) % count, i) for i in range(ends)]),
            ],
            axis=dim,
        )
    return cells


def cut(v):
    hi = v.astype(jnp.bfloat16)
    return hi, (v - hi.astype(jnp.float32)).astype(jnp.bfloat16)


def stacked(v):
    hi, lo = cut(v)
    return jnp.concatenate([hi, lo, hi], axis=0)


def mm(a, b):
    return lax.dot_general(a, b, (((1,), (0,)), ((), ())), preferred_element_type=jnp.float32)


def mm_t(a, b, precision=None):
    return lax.dot_general(
        a, b, (((1,), (1,)), ((), ())), precision=precision, preferred_element_type=jnp.float32
    )


def mm3(a_cut, b):
    hi, lo = cut(b)
    return mm(a_cut[0], hi) + (mm(a_cut[0], lo) + mm(a_cut[1], hi))


def step_kernel(
    nx, ny, modes,
    b_hbm, a_hbm, cols_hbm, s_hbm, n_hbm, map_hbm, inv_hbm,
    precond_ref, image_ref, alpha_ref,
    b_ref, a_ref, cols_ref, s_ref, n_ref, map_ref, inv_ref, loaded,
    blocks, nulls, field, up, down, left, right, local, edge, smoother, info, info_all, near, coarse, coarse_all,
    sums, sums_all, halo_send, halo_recv, near_send, near_recv, col_send, col_recv,
    all_send, all_recv, sum_send, sum_recv,
):
    rows, cols, blk, cases = b_ref.shape
    count = rows * cols
    size = count * blk
    n = nx * ny
    width = info.shape[1]
    coarse_rows = n * 8
    x, y = lax.axis_index("gx"), lax.axis_index("gy")
    me = x * ny + y
    sides = (
        (x > 0, (x - 1, y)),
        (x < nx - 1, (x + 1, y)),
        (y > 0, (x, y - 1)),
        (y < ny - 1, (x, y + 1)),
    )
    halos = (up, down, left, right)

    coarse_all[...] = jnp.zeros_like(coarse_all)
    barrier = pltpu.get_barrier_semaphore()

    def greet(j, carry):
        peer = lax.rem(me + j, n)
        pl.semaphore_signal(
            barrier, inc=1, device_id=(peer // ny, lax.rem(peer, ny)),
            device_id_type=pl.DeviceIdType.MESH,
        )
        return carry

    lax.fori_loop(1, n, greet, 0)

    loads = [
        pltpu.make_async_copy(src, dst, loaded.at[i])
        for i, (src, dst) in enumerate(
            (
                (s_hbm, s_ref), (b_hbm, b_ref), (n_hbm, n_ref), (inv_hbm, inv_ref),
                (map_hbm, map_ref), (cols_hbm, cols_ref), (a_hbm, a_ref),
            )
        )
    ]
    for load in loads:
        load.start()

    def at_column(src, dst, k):
        copies = []
        for j in range(1, ny):
            copies.append(
                pltpu.make_async_remote_copy(
                    src_ref=src, dst_ref=dst.at[me], send_sem=col_send.at[k, j],
                    recv_sem=col_recv.at[k, ny - j],
                    device_id=(x, lax.rem(y + j, ny)), device_id_type=pl.DeviceIdType.MESH,
                )
            )
        return copies

    def pass_on(src, dst, slot, k):
        def one(j, carry):
            pltpu.make_async_remote_copy(
                src_ref=src, dst_ref=dst.at[slot], send_sem=all_send.at[k], recv_sem=all_recv.at[k],
                device_id=(lax.rem(x + j, nx), y), device_id_type=pl.DeviceIdType.MESH,
            ).start()
            return carry

        lax.fori_loop(1, nx, one, 0)

    def gather_start(src, dst, k):
        for copy in at_column(src, dst, k):
            copy.start()
        pass_on(src, dst, me, k)

    def gather_pass(src, dst, k):
        for j in list(range(1, ny, 2)) + list(range(2, ny, 2)):
            slot = x * ny + lax.rem(y + j, ny)
            pltpu.make_async_copy(src, src, col_recv.at[k, j]).wait()
            pass_on(dst.at[slot], dst, slot, k)

    def wait_many(dst, tiles, sem):
        some = dst.at[pl.ds(0, tiles)]
        pltpu.make_async_copy(some, some, sem).wait()

    def gather_end(dst, k):
        wait_many(dst, (nx - 1) * ny, all_recv.at[k])

    def gather_sent(src, dst, k):
        for copy in at_column(src, dst, k):
            copy.wait_send()
        wait_many(dst, (nx - 1) * ny, all_send.at[k])

    def halo_copies(k):
        now = field.at[k]
        out = (
            (now.at[0], down.at[k], 1),
            (now.at[rows - 1], up.at[k], 0),
            (now.at[:, 0], right.at[k], 3),
            (now.at[:, cols - 1], left.at[k], 2),
        )
        return [
            pltpu.make_async_remote_copy(
                src_ref=src, dst_ref=dst,
                send_sem=halo_send.at[k, side], recv_sem=halo_recv.at[k, lands],
                device_id=peer, device_id_type=pl.DeviceIdType.MESH,
            )
            for side, ((src, dst, lands), (_, peer)) in enumerate(zip(out, sides))
        ]

    def halo_start(k):
        for (here, _), copy in zip(sides, halo_copies(k)):
            pl.when(here)(copy.start)

    def halo_wait(k):
        for side, (here, _) in enumerate(sides):
            buf = halos[side].at[k]
            pl.when(here)(pltpu.make_async_copy(buf, buf, halo_recv.at[k, side]).wait)

    def near_copies():
        return [
            pltpu.make_async_remote_copy(
                src_ref=nulls, dst_ref=near.at[lands],
                send_sem=near_send.at[side], recv_sem=near_recv.at[lands],
                device_id=peer, device_id_type=pl.DeviceIdType.MESH,
            )
            for side, (lands, (_, peer)) in enumerate(zip((1, 0, 3, 2), sides))
        ]

    loads[0].wait()
    for i in range(rows):
        for j in range(cols):
            p = i * cols + j
            for c in range(0, blk * blk, 128):
                blocks[p, 0, c // 128 : c // 128 + 1] = s_ref[j, i : i + 1, c : c + 128]
            flat = blocks[p, 0, 0 : blk * blk // 128]
            for half in range(128 // blk):
                blocks[p, 1, pl.ds(half, blk * blk // 128, stride=128 // blk), 0:blk] = flat[
                    :, half * blk : (half + 1) * blk
                ]
    for p in range(count):
        hi, lo = cut(relax_weight * blocks[p, 1, :, 0:blk])
        smoother[p] = jnp.concatenate([hi, hi, lo], axis=1)

    def smooth(v):
        return jnp.concatenate(
            [mm(smoother[p], stacked(v[p * blk : (p + 1) * blk])) for p in range(count)], axis=0
        )

    loads[1].wait()
    b = b_ref[...].reshape(size, cases)
    first = smooth(b)
    field[0] = first.reshape(rows, cols, blk, cases)
    for side, (here, _) in enumerate(sides):

        @pl.when(jnp.logical_not(here))
        def _():
            halos[side][...] = jnp.zeros_like(halos[side])
            near[side] = jnp.zeros_like(near[side])

    for load in loads[2:5]:
        load.wait()
    nulls[...] = jnp.zeros_like(nulls)
    for i in range(rows):
        for j in range(cols):
            p = i * cols + j
            for k in range(modes):
                nulls[k : k + 1, p * blk : (p + 1) * blk] = n_ref[
                    j, i : i + 1, k * blk : (k + 1) * blk
                ]
    info[...] = jnp.zeros_like(info)
    info[0:modes, 0 : inv_ref.shape[1]] = inv_ref[...]
    info[modes : modes + 1, :] = jnp.full((1, width), map_ref[0, 0].astype(jnp.float32))

    pl.semaphore_wait(barrier, n - 1)
    halo_start(0)
    for (here, _), copy in zip(sides, near_copies()):
        pl.when(here)(copy.start)
    gather_start(info, info_all, 0)
    info_all[pl.ds(me, 1)] = info[...][None]

    local[...] = jnp.zeros_like(local)
    loads[5].wait()
    loads[6].wait()
    for i in range(rows):
        for j in range(cols):
            p = i * cols + j
            tiles = [a_ref[i, j, :, s * blk : (s + 1) * blk] for s in range(5)]
            names = [cols_ref[j, i, s] for s in range(5)]
            for d, (di, dj) in enumerate(((0, 0), (-1, 0), (1, 0), (0, -1), (0, 1))):
                e = (i + 1 + di) * (cols + 2) + j + 1 + dj
                tile = tiles[0] * (names[0] == e).astype(jnp.float32)
                for s in range(1, 5):
                    tile = tile + tiles[s] * (names[s] == e).astype(jnp.float32)
                hi, lo = cut(tile)
                ii, jj = i + di, j + dj
                if 0 <= ii < rows and 0 <= jj < cols:
                    q = ii * cols + jj
                    for k, part in enumerate((hi, hi, lo)):
                        at = k * size + q * blk
                        local[p * blk : (p + 1) * blk, at : at + blk] = part
                else:
                    at = (0, j, cols + j, 2 * cols + i, 2 * cols + rows + i)[d]
                    edge[at] = jnp.concatenate([hi, hi, lo], axis=1)

    def places():
        for j in range(cols):
            yield 0, j, j, j
        for j in range(cols):
            yield 1, j, cols + j, (rows - 1) * cols + j
        for i in range(rows):
            yield 2, i, 2 * cols + i, i * cols
        for i in range(rows):
            yield 3, i, 2 * cols + rows + i, i * cols + cols - 1

    def operate(v, k, beside=lambda: None):
        inner = mm(local[...], stacked(v))
        beside()
        parts = [inner[p * blk : (p + 1) * blk] for p in range(count)]
        halo_wait(k)
        for side, at, e, p in places():
            parts[p] = parts[p] + mm(edge[e], stacked(halos[side][k, at]))
        return jnp.concatenate(parts, axis=0)

    own_n = nulls[...]
    own_hi, own_lo = cut(own_n)
    own_cat = jnp.concatenate([own_hi, own_hi, own_lo], axis=1)

    def restrict(v, k):
        g = mm(own_cat, stacked(v))
        coarse[k] = g
        gather_start(mine(k), theirs_all(k), 1 + k)
        coarse_all[k, pl.ds(me, 1)] = g[None]

    def mine(k):
        return coarse.at[k, 0:modes]

    def theirs_all(k):
        return coarse_all.at[k, :, 0:modes]

    r = b - operate(first, 0, lambda: gather_pass(info, info_all, 0))
    restrict(r, 0)

    for side, (here, _) in enumerate(sides):
        buf = near.at[side]
        pl.when(here)(pltpu.make_async_copy(buf, buf, near_recv.at[side]).wait)

    def at_rows(t, v):
        pieces = [jnp.zeros_like(v)] * 6
        pieces[t] = v
        return jnp.concatenate(pieces, axis=0)

    def across(v):
        hi, lo = cut(v)
        return jnp.concatenate([hi, lo, hi], axis=1)

    spread = mm_t(local[...], across(at_rows(0, own_n)))
    parts = [spread[p * blk : (p + 1) * blk] for p in range(count)]
    theirs = [near[side] for side in range(4)]
    facing = (
        lambda at: (rows - 1) * cols + at,
        lambda at: at,
        lambda at: at * cols + cols - 1,
        lambda at: at * cols,
    )
    for side, at, e, p in places():
        q = facing[side](at)
        block = theirs[side][:, q * blk : (q + 1) * blk]
        parts[p] = parts[p] + mm_t(edge[e], across(at_rows(1 + side, block)))
    spread_cut = cut(jnp.concatenate(parts, axis=0))
    eye = (
        lax.broadcasted_iota(jnp.int32, (size, size), 0)
        == lax.broadcasted_iota(jnp.int32, (size, size), 1)
    ).astype(jnp.float32).astype(jnp.bfloat16)
    prolong_cut = tuple(
        mm_t(eye, part).astype(jnp.bfloat16) for part in cut(at_rows(0, own_n))
    )

    gather_pass(mine(0), theirs_all(0), 1)
    gather_end(info_all, 0)
    inv_all = info_all[...].reshape(coarse_rows, width)
    ids = [me] + [
        jnp.clip(px, 0, nx - 1) * ny + jnp.clip(py, 0, ny - 1) for _, (px, py) in sides
    ]
    lane = lax.broadcasted_iota(jnp.int32, (8, coarse_rows), 1)
    row = lax.broadcasted_iota(jnp.int32, (8, coarse_rows), 0)
    pick = []
    for d in ids:
        tile = info_all[pl.ds(d, 1)].reshape(8, width)
        label = jnp.broadcast_to(tile[modes : modes + 1, 0:1], (8, coarse_rows))
        wanted = label * 8.0 + row.astype(jnp.float32)
        hit = jnp.where(lane.astype(jnp.float32) == wanted, 1.0, 0.0)
        pick.append(jnp.where(row < modes, hit, 0.0))
    pick.append(jnp.zeros((8, coarse_rows), jnp.float32))
    picked = lax.dot_general(
        jnp.concatenate(pick, axis=0), inv_all, (((1,), (0,)), ((), ())),
        precision=highest, preferred_element_type=jnp.float32,
    )
    lane3 = lax.broadcasted_iota(jnp.int32, (n, 8, width), 2).astype(jnp.float32)
    row3 = lax.broadcasted_iota(jnp.int32, (n, 8, width), 1)
    labels = jnp.broadcast_to(info_all[...][:, modes : modes + 1, :], (n, 8, width))
    order = jnp.where(lane3 == labels * float(modes) + row3.astype(jnp.float32), 1.0, 0.0)
    order = jnp.where(row3 < modes, order, 0.0).reshape(coarse_rows, width)
    solve_cut = cut(mm_t(picked, order, precision=highest))

    def correct(k):
        gather_end(theirs_all(k), 1 + k)
        h = mm3(solve_cut, coarse_all[k].reshape(coarse_rows, cases))
        return mm3(prolong_cut, h), mm3(spread_cut, h)

    def relax(v, k):
        s = smooth(v)
        field[k] = s.reshape(rows, cols, blk, cases)
        halo_start(k)
        return s, v - operate(s, k)

    up_by, down_by = correct(0)
    precond = first + up_by
    r = r - down_by
    s, r = relax(r, 1)
    precond = precond + s
    s, r = relax(r, 2)
    precond = precond + s
    restrict(r, 1)
    gather_pass(mine(1), theirs_all(1), 2)
    up_by, down_by = correct(1)
    precond = precond + up_by
    r = r - down_by
    s, r = relax(r, 3)
    precond = precond + s

    image = b - r
    sums[...] = jnp.concatenate(
        [
            jnp.sum(b * precond, axis=0, keepdims=True),
            jnp.sum(precond * image, axis=0, keepdims=True),
            jnp.zeros((6, cases), jnp.float32),
        ],
        axis=0,
    )

    def share(j, carry):
        peer = lax.rem(me + j, n)
        pltpu.make_async_remote_copy(
            src_ref=sums.at[0:2], dst_ref=sums_all.at[me, 0:2], send_sem=sum_send, recv_sem=sum_recv,
            device_id=(peer // ny, lax.rem(peer, ny)), device_id_type=pl.DeviceIdType.MESH,
        ).start()
        return carry

    lax.fori_loop(1, n, share, 0)
    sums_all[pl.ds(me, 1)] = sums[...][None]
    precond_ref[...] = precond.reshape(rows, cols, blk, cases)
    image_ref[...] = image.reshape(rows, cols, blk, cases)
    pairs = sums_all.at[:, 0:2]
    wait_many(pairs, n - 1, sum_recv)
    total = jnp.sum(sums_all[:, 0:2], axis=0)
    alpha_ref[...] = total[0:1] / total[1:2]

    for k in range(4):
        for (here, _), copy in zip(sides, halo_copies(k)):
            pl.when(here)(copy.wait_send)
    for (here, _), copy in zip(sides, near_copies()):
        pl.when(here)(copy.wait_send)
    gather_sent(info, info_all, 0)
    gather_sent(mine(0), theirs_all(0), 1)
    gather_sent(mine(1), theirs_all(1), 2)
    wait_many(pairs, n - 1, sum_send)


def fused(
    nx, ny,
    load_cases, matrix_tiles, block_cols, smoother_blocks, near_null, coarse_map, coarse_inverse
):
    rows, cols, blk, cases = load_cases.shape
    count = rows * cols
    modes = near_null.shape[2] // blk
    n = nx * ny
    width = -(-coarse_inverse.shape[1] // 128) * 128
    block_cols = jnp.transpose(block_cols, (1, 0, 2))
    smoother_blocks = jnp.transpose(smoother_blocks, (1, 0, 2))
    near_null = jnp.transpose(near_null, (1, 0, 2))
    vmem = pl.BlockSpec(memory_space=pltpu.VMEM)
    hbm = pl.BlockSpec(memory_space=pltpu.HBM)
    f32, bf16 = jnp.float32, jnp.bfloat16
    shape = jax.ShapeDtypeStruct(load_cases.shape, f32)
    precond, image, alpha = pl.pallas_call(
        functools.partial(step_kernel, nx, ny, modes),
        out_shape=(shape, shape, jax.ShapeDtypeStruct((1, cases), f32)),
        in_specs=[hbm] * 7,
        out_specs=(vmem, vmem, vmem),
        scratch_shapes=[
            pltpu.VMEM(load_cases.shape, f32),
            pltpu.VMEM(matrix_tiles.shape, f32),
            pltpu.SMEM(block_cols.shape, jnp.int32),
            pltpu.VMEM(smoother_blocks.shape, f32),
            pltpu.VMEM(near_null.shape, f32),
            pltpu.SMEM(coarse_map.shape, jnp.int32),
            pltpu.VMEM(coarse_inverse.shape, f32),
            pltpu.SemaphoreType.DMA((7,)),
            pltpu.VMEM((count, 2, blk, 128), f32),
            pltpu.VMEM((8, count * blk), f32),
            pltpu.VMEM((4, rows, cols, blk, cases), f32),
            pltpu.VMEM((4, cols, blk, cases), f32),
            pltpu.VMEM((4, cols, blk, cases), f32),
            pltpu.VMEM((4, rows, blk, cases), f32),
            pltpu.VMEM((4, rows, blk, cases), f32),
            pltpu.VMEM((count * blk, 3 * count * blk), bf16),
            pltpu.VMEM((2 * (rows + cols), blk, 3 * blk), bf16),
            pltpu.VMEM((count, blk, 3 * blk), bf16),
            pltpu.VMEM((8, width), f32),
            pltpu.VMEM((n, 8, width), f32),
            pltpu.VMEM((4, 8, count * blk), f32),
            pltpu.VMEM((2, 8, cases), f32),
            pltpu.VMEM((2, n, 8, cases), f32),
            pltpu.VMEM((8, cases), f32),
            pltpu.VMEM((n, 8, cases), f32),
            pltpu.SemaphoreType.DMA((4, 4)),
            pltpu.SemaphoreType.DMA((4, 4)),
            pltpu.SemaphoreType.DMA((4,)),
            pltpu.SemaphoreType.DMA((4,)),
            pltpu.SemaphoreType.DMA((3, ny)),
            pltpu.SemaphoreType.DMA((3, ny)),
            pltpu.SemaphoreType.DMA((3,)),
            pltpu.SemaphoreType.DMA((3,)),
            pltpu.SemaphoreType.DMA,
            pltpu.SemaphoreType.DMA,
        ],
        compiler_params=pltpu.CompilerParams(
            collective_id=0, has_side_effects=True, vmem_limit_bytes=60 * 2**20
        ),
    )(
        load_cases, matrix_tiles, block_cols, smoother_blocks, near_null, coarse_map,
        coarse_inverse,
    )
    alpha = alpha.reshape(1, 1, 1, cases)
    return alpha * precond, load_cases - alpha * image


def per_device(
    load_cases, matrix_tiles, block_cols, smoother_blocks, near_null, coarse_map, coarse_inverse
):
    agg_rows, agg_cols, block_size, case_count = load_cases.shape
    mode_count = near_null.shape[2] // block_size
    coarse_total = coarse_inverse.shape[1]
    coarse_aggs = coarse_total // mode_count
    modes = near_null.reshape(agg_rows, agg_cols, mode_count, block_size)
    inverse_blocks = smoother_blocks.reshape(agg_rows, agg_cols, block_size, block_size)

    def operate(vector_field):
        extended = padded(vector_field, (("gx", 0), ("gy", 1)), 1)
        flattened = extended.reshape(-1, block_size, case_count)
        picked = flattened[block_cols].reshape(agg_rows, agg_cols, -1, case_count)
        return jnp.einsum("ijbk,ijkr->ijbr", matrix_tiles, picked, precision=highest)

    def smooth(defect):
        return relax_weight * jnp.einsum(
            "ijab,ijbr->ijar", inverse_blocks, defect, precision=highest
        )

    def correct(defect):
        contrib = jnp.einsum("ijkb,ijbr->ijkr", modes, defect, precision=highest)
        own_part = jnp.sum(contrib, axis=(0, 1))
        my_label = coarse_map[0, 0]
        label_value = jnp.reshape(my_label.astype(jnp.float32), (1,))
        pieces, labels = (
            lax.all_gather(own_part[None], ("gx", "gy"), axis=0, tiled=True),
            lax.all_gather(label_value, ("gx", "gy"), axis=0, tiled=True),
        )
        label_ids = labels.astype(jnp.int32)
        placing = (label_ids[:, None] == jnp.arange(coarse_aggs, dtype=jnp.int32)[None, :]).astype(
            jnp.float32
        )
        ordered = jnp.einsum("dc,dkr->ckr", placing, pieces, precision=highest).reshape(
            coarse_total, case_count
        )
        own_rows = jnp.dot(coarse_inverse, ordered, precision=highest)
        solved = lax.all_gather(own_rows, ("gx", "gy"), axis=0, tiled=True)
        mine = lax.dynamic_slice_in_dim(solved, my_label * mode_count, mode_count, 0)
        coarse_back = jnp.broadcast_to(
            mine[None, None], (agg_rows, agg_cols, mode_count, case_count)
        )
        return jnp.einsum("ijkb,ijkr->ijbr", modes, coarse_back, precision=highest)

    first = smooth(load_cases)
    first = first + correct(load_cases - operate(first))
    precond = first + smooth(load_cases - operate(first))
    defect = load_cases - operate(precond)
    update = smooth(defect)
    update = update + correct(defect - operate(update))
    update = update + smooth(defect - operate(update))
    precond = precond + update
    local_aligned = jnp.sum(load_cases * precond, axis=(0, 1, 2))
    aligned = lax.psum(local_aligned, ("gx", "gy"))
    image = operate(precond)
    curved = lax.psum(jnp.sum(precond * image, axis=(0, 1, 2)), ("gx", "gy"))
    alpha = aligned / curved
    solution = alpha * precond
    residual = load_cases - alpha * image
    return (solution, residual)


def solution(mesh):
    nx, ny = mesh.shape["gx"], mesh.shape["gy"]
    step = functools.partial(fused, nx, ny) if nx * ny <= 128 else per_device
    placed = (
        P("gx", "gy", None, None),
        P("gx", "gy", None, None),
        P("gx", "gy", None),
        P("gx", "gy", None),
        P("gx", "gy", None),
        P("gx", "gy"),
        P(("gx", "gy"), None),
    )
    return jax.shard_map(
        step,
        mesh=mesh,
        in_specs=placed,
        out_specs=(P("gx", "gy", None, None), P("gx", "gy", None, None)),
        check_vma=False,
    )
```

```python
import functools

import jax
import jax.numpy as jnp
from jax import lax
from jax.experimental import pallas as pl
from jax.experimental.pallas import tpu as pltpu
from jax.sharding import PartitionSpec as P

relax_weight = 0.8
highest = lax.Precision.HIGHEST


def padded(cells, sides, width):
    for axis, dim in sides:
        count = lax.axis_size(axis)
        ends = count - 1
        head = lax.slice_in_dim(cells, 0, width, axis=dim)
        tail = lax.slice_in_dim(cells, cells.shape[dim] - width, cells.shape[dim], axis=dim)
        cells = jnp.concatenate(
            [
                lax.ppermute(tail, axis, [(i, (i + 1) % count) for i in range(ends)]),
                cells,
                lax.ppermute(head, axis, [((i + 1) % count, i) for i in range(ends)]),
            ],
            axis=dim,
        )
    return cells


def cut(v):
    hi = v.astype(jnp.bfloat16)
    return hi, (v - hi.astype(jnp.float32)).astype(jnp.bfloat16)


def stacked(v):
    hi, lo = cut(v)
    return jnp.concatenate([hi, lo, hi], axis=0)


def mm(a, b):
    return lax.dot_general(a, b, (((1,), (0,)), ((), ())), preferred_element_type=jnp.float32)


def mm_t(a, b, precision=None):
    return lax.dot_general(
        a, b, (((1,), (1,)), ((), ())), precision=precision, preferred_element_type=jnp.float32
    )


def mm3(a_cut, b):
    hi, lo = cut(b)
    return mm(a_cut[0], hi) + (mm(a_cut[0], lo) + mm(a_cut[1], hi))


def step_kernel(
    nx, ny, modes,
    b_hbm, a_hbm, cols_hbm, s_hbm, n_hbm, map_hbm, inv_hbm,
    precond_ref, image_ref, alpha_ref,
    b_ref, a_ref, cols_ref, s_ref, n_ref, map_ref, inv_ref, loaded,
    blocks, nulls, field, up, down, left, right, local, edge, smoother, info, info_all, near, coarse, coarse_all,
    sums, sums_all, halo_send, halo_recv, near_send, near_recv, col_send, col_recv,
    all_send, all_recv, sum_send, sum_recv,
):
    rows, cols, blk, cases = b_ref.shape
    count = rows * cols
    size = count * blk
    n = nx * ny
    width = info.shape[1]
    coarse_rows = n * 8
    x, y = lax.axis_index("gx"), lax.axis_index("gy")
    me = x * ny + y
    sides = (
        (x > 0, (x - 1, y)),
        (x < nx - 1, (x + 1, y)),
        (y > 0, (x, y - 1)),
        (y < ny - 1, (x, y + 1)),
    )
    halos = (up, down, left, right)

    coarse_all[...] = jnp.zeros_like(coarse_all)
    barrier = pltpu.get_barrier_semaphore()

    def greet(j, carry):
        peer = lax.rem(me + j, n)
        pl.semaphore_signal(
            barrier, inc=1, device_id=(peer // ny, lax.rem(peer, ny)),
            device_id_type=pl.DeviceIdType.MESH,
        )
        return carry

    lax.fori_loop(1, n, greet, 0)

    loads = [
        pltpu.make_async_copy(src, dst, loaded.at[i])
        for i, (src, dst) in enumerate(
            (
                (s_hbm, s_ref), (b_hbm, b_ref), (n_hbm, n_ref), (inv_hbm, inv_ref),
                (map_hbm, map_ref), (cols_hbm, cols_ref), (a_hbm, a_ref),
            )
        )
    ]
    for load in loads:
        load.start()

    def at_column(src, dst, k):
        copies = []
        for j in range(1, ny):
            copies.append(
                pltpu.make_async_remote_copy(
                    src_ref=src, dst_ref=dst.at[me], send_sem=col_send.at[k, j],
                    recv_sem=col_recv.at[k, ny - j],
                    device_id=(x, lax.rem(y + j, ny)), device_id_type=pl.DeviceIdType.MESH,
                )
            )
        return copies

    def pass_on(src, dst, slot, k):
        def one(j, carry):
            pltpu.make_async_remote_copy(
                src_ref=src, dst_ref=dst.at[slot], send_sem=all_send.at[k], recv_sem=all_recv.at[k],
                device_id=(lax.rem(x + j, nx), y), device_id_type=pl.DeviceIdType.MESH,
            ).start()
            return carry

        lax.fori_loop(1, nx, one, 0)

    def gather_start(src, dst, k):
        for copy in at_column(src, dst, k):
            copy.start()
        pass_on(src, dst, me, k)

    def gather_pass(src, dst, k):
        for j in list(range(1, ny, 2)) + list(range(2, ny, 2)):
            slot = x * ny + lax.rem(y + j, ny)
            pltpu.make_async_copy(src, src, col_recv.at[k, j]).wait()
            pass_on(dst.at[slot], dst, slot, k)

    def wait_many(dst, tiles, sem):
        some = dst.at[pl.ds(0, tiles)]
        pltpu.make_async_copy(some, some, sem).wait()

    def gather_end(dst, k):
        wait_many(dst, (nx - 1) * ny, all_recv.at[k])

    def gather_sent(src, dst, k):
        for copy in at_column(src, dst, k):
            copy.wait_send()
        wait_many(dst, (nx - 1) * ny, all_send.at[k])

    def halo_copies(k):
        now = field.at[k]
        out = (
            (now.at[0], down.at[k], 1),
            (now.at[rows - 1], up.at[k], 0),
            (now.at[:, 0], right.at[k], 3),
            (now.at[:, cols - 1], left.at[k], 2),
        )
        return [
            pltpu.make_async_remote_copy(
                src_ref=src, dst_ref=dst,
                send_sem=halo_send.at[k, side], recv_sem=halo_recv.at[k, lands],
                device_id=peer, device_id_type=pl.DeviceIdType.MESH,
            )
            for side, ((src, dst, lands), (_, peer)) in enumerate(zip(out, sides))
        ]

    def halo_start(k):
        for (here, _), copy in zip(sides, halo_copies(k)):
            pl.when(here)(copy.start)

    def halo_wait(k, side):
        buf = halos[side].at[k]
        pl.when(sides[side][0])(pltpu.make_async_copy(buf, buf, halo_recv.at[k, side]).wait)

    def near_copies():
        return [
            pltpu.make_async_remote_copy(
                src_ref=nulls, dst_ref=near.at[lands],
                send_sem=near_send.at[side], recv_sem=near_recv.at[lands],
                device_id=peer, device_id_type=pl.DeviceIdType.MESH,
            )
            for side, (lands, (_, peer)) in enumerate(zip((1, 0, 3, 2), sides))
        ]

    loads[0].wait()
    for i in range(rows):
        for j in range(cols):
            p = i * cols + j
            for c in range(0, blk * blk, 128):
                blocks[p, 0, c // 128 : c // 128 + 1] = s_ref[j, i : i + 1, c : c + 128]
            flat = blocks[p, 0, 0 : blk * blk // 128]
            for half in range(128 // blk):
                blocks[p, 1, pl.ds(half, blk * blk // 128, stride=128 // blk), 0:blk] = flat[
                    :, half * blk : (half + 1) * blk
                ]
    for p in range(count):
        hi, lo = cut(relax_weight * blocks[p, 1, :, 0:blk])
        smoother[p] = jnp.concatenate([hi, hi, lo], axis=1)

    def smooth(v):
        return jnp.concatenate(
            [mm(smoother[p], stacked(v[p * blk : (p + 1) * blk])) for p in range(count)], axis=0
        )

    loads[1].wait()
    b = b_ref[...].reshape(size, cases)
    first = smooth(b)
    field[0] = first.reshape(rows, cols, blk, cases)
    for side, (here, _) in enumerate(sides):

        @pl.when(jnp.logical_not(here))
        def _():
            halos[side][...] = jnp.zeros_like(halos[side])
            near[side] = jnp.zeros_like(near[side])

    for load in loads[2:5]:
        load.wait()
    nulls[...] = jnp.zeros_like(nulls)
    for i in range(rows):
        for j in range(cols):
            p = i * cols + j
            for k in range(modes):
                nulls[k : k + 1, p * blk : (p + 1) * blk] = n_ref[
                    j, i : i + 1, k * blk : (k + 1) * blk
                ]
    info[...] = jnp.zeros_like(info)
    info[0:modes, 0 : inv_ref.shape[1]] = inv_ref[...]
    info[modes : modes + 1, :] = jnp.full((1, width), map_ref[0, 0].astype(jnp.float32))

    local[...] = jnp.zeros_like(local)
    loads[5].wait()
    loads[6].wait()
    for i in range(rows):
        for j in range(cols):
            p = i * cols + j
            tiles = [a_ref[i, j, :, s * blk : (s + 1) * blk] for s in range(5)]
            names = [cols_ref[j, i, s] for s in range(5)]
            for d, (di, dj) in enumerate(((0, 0), (-1, 0), (1, 0), (0, -1), (0, 1))):
                e = (i + 1 + di) * (cols + 2) + j + 1 + dj
                tile = tiles[0] * (names[0] == e).astype(jnp.float32)
                for s in range(1, 5):
                    tile = tile + tiles[s] * (names[s] == e).astype(jnp.float32)
                hi, lo = cut(tile)
                ii, jj = i + di, j + dj
                if 0 <= ii < rows and 0 <= jj < cols:
                    q = ii * cols + jj
                    for k, part in enumerate((hi, hi, lo)):
                        at = k * size + q * blk
                        local[p * blk : (p + 1) * blk, at : at + blk] = part
                else:
                    at = (0, j, cols + j, 2 * cols + i, 2 * cols + rows + i)[d]
                    edge[at] = jnp.concatenate([hi, hi, lo], axis=1)

    pl.semaphore_wait(barrier, n - 1)
    halo_start(0)
    for (here, _), copy in zip(sides, near_copies()):
        pl.when(here)(copy.start)
    gather_start(info, info_all, 0)
    info_all[pl.ds(me, 1)] = info[...][None]

    def places():
        for j in range(cols):
            yield 0, j, j, j
        for j in range(cols):
            yield 1, j, cols + j, (rows - 1) * cols + j
        for i in range(rows):
            yield 2, i, 2 * cols + i, i * cols
        for i in range(rows):
            yield 3, i, 2 * cols + rows + i, i * cols + cols - 1

    def operate(v, k):
        inner = mm(local[...], stacked(v))
        parts = [inner[p * blk : (p + 1) * blk] for p in range(count)]
        for side in (2, 3, 0, 1):
            halo_wait(k, side)
            for at_side, at, e, p in places():
                if at_side == side:
                    parts[p] = parts[p] + mm(edge[e], stacked(halos[side][k, at]))
        return jnp.concatenate(parts, axis=0)

    own_n = nulls[...]
    own_hi, own_lo = cut(own_n)
    own_cat = jnp.concatenate([own_hi, own_hi, own_lo], axis=1)

    def restrict(v, k):
        g = mm(own_cat, stacked(v))
        coarse[k] = g
        gather_start(mine(k), theirs_all(k), 1 + k)
        coarse_all[k, pl.ds(me, 1)] = g[None]

    def mine(k):
        return coarse.at[k, 0:modes]

    def theirs_all(k):
        return coarse_all.at[k, :, 0:modes]

    r = b - operate(first, 0)
    restrict(r, 0)
    gather_pass(info, info_all, 0)

    for side, (here, _) in enumerate(sides):
        buf = near.at[side]
        pl.when(here)(pltpu.make_async_copy(buf, buf, near_recv.at[side]).wait)

    def at_rows(t, v):
        pieces = [jnp.zeros_like(v)] * 6
        pieces[t] = v
        return jnp.concatenate(pieces, axis=0)

    def across(v):
        hi, lo = cut(v)
        return jnp.concatenate([hi, lo, hi], axis=1)

    spread = mm_t(local[...], across(at_rows(0, own_n)))
    parts = [spread[p * blk : (p + 1) * blk] for p in range(count)]
    theirs = [near[side] for side in range(4)]
    facing = (
        lambda at: (rows - 1) * cols + at,
        lambda at: at,
        lambda at: at * cols + cols - 1,
        lambda at: at * cols,
    )
    for side, at, e, p in places():
        q = facing[side](at)
        block = theirs[side][:, q * blk : (q + 1) * blk]
        parts[p] = parts[p] + mm_t(edge[e], across(at_rows(1 + side, block)))
    spread = jnp.concatenate(parts, axis=0)
    eye = (
        lax.broadcasted_iota(jnp.int32, (size, size), 0)
        == lax.broadcasted_iota(jnp.int32, (size, size), 1)
    ).astype(jnp.float32).astype(jnp.bfloat16)
    prolong_cut = tuple(
        mm_t(eye, part).astype(jnp.bfloat16) for part in cut(at_rows(0, own_n))
    )

    gather_pass(mine(0), theirs_all(0), 1)
    gather_end(info_all, 0)
    inv_all = info_all[...].reshape(coarse_rows, width)
    ids = [me] + [
        jnp.clip(px, 0, nx - 1) * ny + jnp.clip(py, 0, ny - 1) for _, (px, py) in sides
    ]
    lane = lax.broadcasted_iota(jnp.int32, (8, coarse_rows), 1)
    row = lax.broadcasted_iota(jnp.int32, (8, coarse_rows), 0)
    pick = []
    for d in ids:
        tile = info_all[pl.ds(d, 1)].reshape(8, width)
        label = jnp.broadcast_to(tile[modes : modes + 1, 0:1], (8, coarse_rows))
        wanted = label * 8.0 + row.astype(jnp.float32)
        hit = jnp.where(lane.astype(jnp.float32) == wanted, 1.0, 0.0)
        pick.append(jnp.where(row < modes, hit, 0.0))
    pick.append(jnp.zeros((8, coarse_rows), jnp.float32))
    picked = lax.dot_general(
        jnp.concatenate(pick, axis=0), inv_all, (((1,), (0,)), ((), ())),
        precision=highest, preferred_element_type=jnp.float32,
    )
    lane3 = lax.broadcasted_iota(jnp.int32, (n, 8, width), 2).astype(jnp.float32)
    row3 = lax.broadcasted_iota(jnp.int32, (n, 8, width), 1)
    labels = jnp.broadcast_to(info_all[...][:, modes : modes + 1, :], (n, 8, width))
    order = jnp.where(lane3 == labels * float(modes) + row3.astype(jnp.float32), 1.0, 0.0)
    order = jnp.where(row3 < modes, order, 0.0).reshape(coarse_rows, width)
    solve = mm_t(picked, order, precision=highest)
    solve_cut = cut(solve)
    spread_cut = cut(mm3(cut(spread), solve))

    def correct(k):
        gather_end(theirs_all(k), 1 + k)
        g = coarse_all[k].reshape(coarse_rows, cases)
        return mm3(prolong_cut, mm3(solve_cut, g)), mm3(spread_cut, g)

    def relax(v, k):
        s = smooth(v)
        field[k] = s.reshape(rows, cols, blk, cases)
        halo_start(k)
        return s, v - operate(s, k)

    up_by, down_by = correct(0)
    precond = first + up_by
    r = r - down_by
    s, r = relax(r, 1)
    precond = precond + s
    s, r = relax(r, 2)
    precond = precond + s
    restrict(r, 1)
    gather_pass(mine(1), theirs_all(1), 2)
    up_by, down_by = correct(1)
    precond = precond + up_by
    r = r - down_by
    s, r = relax(r, 3)
    precond = precond + s

    image = b - r
    sums[...] = jnp.concatenate(
        [
            jnp.sum(b * precond, axis=0, keepdims=True),
            jnp.sum(precond * image, axis=0, keepdims=True),
            jnp.zeros((6, cases), jnp.float32),
        ],
        axis=0,
    )

    def share(j, carry):
        peer = lax.rem(me + j, n)
        pltpu.make_async_remote_copy(
            src_ref=sums.at[0:2], dst_ref=sums_all.at[me, 0:2], send_sem=sum_send, recv_sem=sum_recv,
            device_id=(peer // ny, lax.rem(peer, ny)), device_id_type=pl.DeviceIdType.MESH,
        ).start()
        return carry

    lax.fori_loop(1, n, share, 0)
    sums_all[pl.ds(me, 1)] = sums[...][None]
    precond_ref[...] = precond.reshape(rows, cols, blk, cases)
    image_ref[...] = image.reshape(rows, cols, blk, cases)
    pairs = sums_all.at[:, 0:2]
    wait_many(pairs, n - 1, sum_recv)
    total = jnp.sum(sums_all[:, 0:2], axis=0)
    alpha_ref[...] = total[0:1] / total[1:2]

    for k in range(4):
        for (here, _), copy in zip(sides, halo_copies(k)):
            pl.when(here)(copy.wait_send)
    for (here, _), copy in zip(sides, near_copies()):
        pl.when(here)(copy.wait_send)
    gather_sent(info, info_all, 0)
    gather_sent(mine(0), theirs_all(0), 1)
    gather_sent(mine(1), theirs_all(1), 2)
    wait_many(pairs, n - 1, sum_send)


def finish_kernel(b_ref, p_ref, i_ref, alpha_ref, sol_ref, res_ref, held, scale, sems, scale_sem):
    rows = b_ref.shape[0]
    first = pltpu.make_async_copy(alpha_ref, scale, scale_sem)
    first.start()

    def move(k, i):
        ref = (p_ref, i_ref, b_ref, sol_ref, res_ref)[k]
        ends = (ref.at[i], held.at[k, i])
        return pltpu.make_async_copy(*(ends if k < 3 else ends[::-1]), sems.at[k, i])

    for i in range(rows):
        for k in range(3):
            move(k, i).start()
    first.wait()
    alpha = scale[...].reshape(1, 1, -1)
    for i in range(rows):
        move(0, i).wait()
        held[3, i] = alpha * held[0, i]
        move(3, i).start()
        move(1, i).wait()
        move(2, i).wait()
        held[4, i] = held[2, i] - alpha * held[1, i]
        move(4, i).start()
    for i in range(rows):
        move(3, i).wait()
        move(4, i).wait()


def fused(
    nx, ny,
    load_cases, matrix_tiles, block_cols, smoother_blocks, near_null, coarse_map, coarse_inverse
):
    rows, cols, blk, cases = load_cases.shape
    count = rows * cols
    modes = near_null.shape[2] // blk
    n = nx * ny
    width = -(-coarse_inverse.shape[1] // 128) * 128
    block_cols = jnp.transpose(block_cols, (1, 0, 2))
    smoother_blocks = jnp.transpose(smoother_blocks, (1, 0, 2))
    near_null = jnp.transpose(near_null, (1, 0, 2))
    vmem = pl.BlockSpec(memory_space=pltpu.VMEM)
    hbm = pl.BlockSpec(memory_space=pltpu.HBM)
    f32, bf16 = jnp.float32, jnp.bfloat16
    shape = jax.ShapeDtypeStruct(load_cases.shape, f32)
    precond, image, alpha = pl.pallas_call(
        functools.partial(step_kernel, nx, ny, modes),
        out_shape=(shape, shape, jax.ShapeDtypeStruct((1, cases), f32)),
        in_specs=[hbm] * 7,
        out_specs=(vmem, vmem, vmem),
        scratch_shapes=[
            pltpu.VMEM(load_cases.shape, f32),
            pltpu.VMEM(matrix_tiles.shape, f32),
            pltpu.SMEM(block_cols.shape, jnp.int32),
            pltpu.VMEM(smoother_blocks.shape, f32),
            pltpu.VMEM(near_null.shape, f32),
            pltpu.SMEM(coarse_map.shape, jnp.int32),
            pltpu.VMEM(coarse_inverse.shape, f32),
            pltpu.SemaphoreType.DMA((7,)),
            pltpu.VMEM((count, 2, blk, 128), f32),
            pltpu.VMEM((8, count * blk), f32),
            pltpu.VMEM((4, rows, cols, blk, cases), f32),
            pltpu.VMEM((4, cols, blk, cases), f32),
            pltpu.VMEM((4, cols, blk, cases), f32),
            pltpu.VMEM((4, rows, blk, cases), f32),
            pltpu.VMEM((4, rows, blk, cases), f32),
            pltpu.VMEM((count * blk, 3 * count * blk), bf16),
            pltpu.VMEM((2 * (rows + cols), blk, 3 * blk), bf16),
            pltpu.VMEM((count, blk, 3 * blk), bf16),
            pltpu.VMEM((8, width), f32),
            pltpu.VMEM((n, 8, width), f32),
            pltpu.VMEM((4, 8, count * blk), f32),
            pltpu.VMEM((2, 8, cases), f32),
            pltpu.VMEM((2, n, 8, cases), f32),
            pltpu.VMEM((8, cases), f32),
            pltpu.VMEM((n, 8, cases), f32),
            pltpu.SemaphoreType.DMA((4, 4)),
            pltpu.SemaphoreType.DMA((4, 4)),
            pltpu.SemaphoreType.DMA((4,)),
            pltpu.SemaphoreType.DMA((4,)),
            pltpu.SemaphoreType.DMA((3, ny)),
            pltpu.SemaphoreType.DMA((3, ny)),
            pltpu.SemaphoreType.DMA((3,)),
            pltpu.SemaphoreType.DMA((3,)),
            pltpu.SemaphoreType.DMA,
            pltpu.SemaphoreType.DMA,
        ],
        compiler_params=pltpu.CompilerParams(
            collective_id=0, has_side_effects=True, vmem_limit_bytes=60 * 2**20
        ),
    )(
        load_cases, matrix_tiles, block_cols, smoother_blocks, near_null, coarse_map,
        coarse_inverse,
    )
    return pl.pallas_call(
        finish_kernel,
        out_shape=(shape, shape),
        in_specs=[hbm, hbm, hbm, hbm],
        out_specs=(hbm, hbm),
        scratch_shapes=[
            pltpu.VMEM((5,) + load_cases.shape, f32),
            pltpu.VMEM((1, cases), f32),
            pltpu.SemaphoreType.DMA((5, rows)),
            pltpu.SemaphoreType.DMA,
        ],
        compiler_params=pltpu.CompilerParams(vmem_limit_bytes=60 * 2**20),
    )(load_cases, precond, image, alpha)


def per_device(
    load_cases, matrix_tiles, block_cols, smoother_blocks, near_null, coarse_map, coarse_inverse
):
    agg_rows, agg_cols, block_size, case_count = load_cases.shape
    mode_count = near_null.shape[2] // block_size
    coarse_total = coarse_inverse.shape[1]
    coarse_aggs = coarse_total // mode_count
    modes = near_null.reshape(agg_rows, agg_cols, mode_count, block_size)
    inverse_blocks = smoother_blocks.reshape(agg_rows, agg_cols, block_size, block_size)

    def operate(vector_field):
        extended = padded(vector_field, (("gx", 0), ("gy", 1)), 1)
        flattened = extended.reshape(-1, block_size, case_count)
        picked = flattened[block_cols].reshape(agg_rows, agg_cols, -1, case_count)
        return jnp.einsum("ijbk,ijkr->ijbr", matrix_tiles, picked, precision=highest)

    def smooth(defect):
        return relax_weight * jnp.einsum(
            "ijab,ijbr->ijar", inverse_blocks, defect, precision=highest
        )

    def correct(defect):
        contrib = jnp.einsum("ijkb,ijbr->ijkr", modes, defect, precision=highest)
        own_part = jnp.sum(contrib, axis=(0, 1))
        my_label = coarse_map[0, 0]
        label_value = jnp.reshape(my_label.astype(jnp.float32), (1,))
        pieces, labels = (
            lax.all_gather(own_part[None], ("gx", "gy"), axis=0, tiled=True),
            lax.all_gather(label_value, ("gx", "gy"), axis=0, tiled=True),
        )
        label_ids = labels.astype(jnp.int32)
        placing = (label_ids[:, None] == jnp.arange(coarse_aggs, dtype=jnp.int32)[None, :]).astype(
            jnp.float32
        )
        ordered = jnp.einsum("dc,dkr->ckr", placing, pieces, precision=highest).reshape(
            coarse_total, case_count
        )
        own_rows = jnp.dot(coarse_inverse, ordered, precision=highest)
        solved = lax.all_gather(own_rows, ("gx", "gy"), axis=0, tiled=True)
        mine = lax.dynamic_slice_in_dim(solved, my_label * mode_count, mode_count, 0)
        coarse_back = jnp.broadcast_to(
            mine[None, None], (agg_rows, agg_cols, mode_count, case_count)
        )
        return jnp.einsum("ijkb,ijkr->ijbr", modes, coarse_back, precision=highest)

    first = smooth(load_cases)
    first = first + correct(load_cases - operate(first))
    precond = first + smooth(load_cases - operate(first))
    defect = load_cases - operate(precond)
    update = smooth(defect)
    update = update + correct(defect - operate(update))
    update = update + smooth(defect - operate(update))
    precond = precond + update
    local_aligned = jnp.sum(load_cases * precond, axis=(0, 1, 2))
    aligned = lax.psum(local_aligned, ("gx", "gy"))
    image = operate(precond)
    curved = lax.psum(jnp.sum(precond * image, axis=(0, 1, 2)), ("gx", "gy"))
    alpha = aligned / curved
    solution = alpha * precond
    residual = load_cases - alpha * image
    return (solution, residual)


def solution(mesh):
    nx, ny = mesh.shape["gx"], mesh.shape["gy"]
    step = functools.partial(fused, nx, ny) if nx * ny <= 128 else per_device
    placed = (
        P("gx", "gy", None, None),
        P("gx", "gy", None, None),
        P("gx", "gy", None),
        P("gx", "gy", None),
        P("gx", "gy", None),
        P("gx", "gy"),
        P(("gx", "gy"), None),
    )
    return jax.shard_map(
        step,
        mesh=mesh,
        in_specs=placed,
        out_specs=(P("gx", "gy", None, None), P("gx", "gy", None, None)),
        check_vma=False,
    )
```

```python
import functools

import jax
import jax.numpy as jnp
from jax import lax
from jax.experimental import pallas as pl
from jax.experimental.pallas import tpu as pltpu
from jax.sharding import PartitionSpec as P

relax_weight = 0.8
highest = lax.Precision.HIGHEST


def padded(cells, sides, width):
    for axis, dim in sides:
        count = lax.axis_size(axis)
        ends = count - 1
        head = lax.slice_in_dim(cells, 0, width, axis=dim)
        tail = lax.slice_in_dim(cells, cells.shape[dim] - width, cells.shape[dim], axis=dim)
        cells = jnp.concatenate(
            [
                lax.ppermute(tail, axis, [(i, (i + 1) % count) for i in range(ends)]),
                cells,
                lax.ppermute(head, axis, [((i + 1) % count, i) for i in range(ends)]),
            ],
            axis=dim,
        )
    return cells


def cut(v):
    hi = v.astype(jnp.bfloat16)
    return hi, (v - hi.astype(jnp.float32)).astype(jnp.bfloat16)


def stacked(v):
    hi, lo = cut(v)
    return jnp.concatenate([hi, lo, hi], axis=0)


def mm(a, b):
    return lax.dot_general(a, b, (((1,), (0,)), ((), ())), preferred_element_type=jnp.float32)


def mm_t(a, b, precision=None):
    return lax.dot_general(
        a, b, (((1,), (1,)), ((), ())), precision=precision, preferred_element_type=jnp.float32
    )


def mm3(a_cut, b):
    hi, lo = cut(b)
    return mm(a_cut[0], hi) + (mm(a_cut[0], lo) + mm(a_cut[1], hi))


def step_kernel(
    nx, ny, modes,
    b_hbm, a_hbm, cols_hbm, s_hbm, n_hbm, map_hbm, inv_hbm,
    precond_ref, image_ref, alpha_ref,
    b_ref, a_ref, cols_ref, s_ref, n_ref, map_ref, inv_ref, loaded,
    blocks, nulls, field, up, down, left, right, local, edge, smoother, info, info_all, near, coarse, coarse_all,
    sums, sums_all, halo_send, halo_recv, near_send, near_recv, col_send, col_recv,
    all_send, all_recv, sum_send, sum_recv,
):
    rows, cols, blk, cases = b_ref.shape
    count = rows * cols
    size = count * blk
    n = nx * ny
    width = info.shape[1]
    coarse_rows = n * 8
    x, y = lax.axis_index("gx"), lax.axis_index("gy")
    me = x * ny + y
    sides = (
        (x > 0, (x - 1, y)),
        (x < nx - 1, (x + 1, y)),
        (y > 0, (x, y - 1)),
        (y < ny - 1, (x, y + 1)),
    )
    halos = (up, down, left, right)

    coarse_all[...] = jnp.zeros_like(coarse_all)
    info_all[...] = jnp.zeros_like(info_all)
    told, told_all = info.at[0 : modes + 1], info_all.at[:, 0 : modes + 1]
    barrier = pltpu.get_barrier_semaphore()

    def greet(j, carry):
        peer = lax.rem(me + j, n)
        pl.semaphore_signal(
            barrier, inc=1, device_id=(peer // ny, lax.rem(peer, ny)),
            device_id_type=pl.DeviceIdType.MESH,
        )
        return carry

    lax.fori_loop(1, n, greet, 0)

    loads = [
        pltpu.make_async_copy(src, dst, loaded.at[i])
        for i, (src, dst) in enumerate(
            (
                (s_hbm, s_ref), (b_hbm, b_ref), (n_hbm, n_ref), (inv_hbm, inv_ref),
                (map_hbm, map_ref), (cols_hbm, cols_ref), (a_hbm, a_ref),
            )
        )
    ]
    for load in loads:
        load.start()

    def at_column(src, dst, k):
        copies = []
        for j in range(1, ny):
            copies.append(
                pltpu.make_async_remote_copy(
                    src_ref=src, dst_ref=dst.at[me], send_sem=col_send.at[k, j],
                    recv_sem=col_recv.at[k, ny - j],
                    device_id=(x, lax.rem(y + j, ny)), device_id_type=pl.DeviceIdType.MESH,
                )
            )
        return copies

    def pass_on(src, dst, slot, k):
        def one(j, carry):
            pltpu.make_async_remote_copy(
                src_ref=src, dst_ref=dst.at[slot], send_sem=all_send.at[k], recv_sem=all_recv.at[k],
                device_id=(lax.rem(x + j, nx), y), device_id_type=pl.DeviceIdType.MESH,
            ).start()
            return carry

        lax.fori_loop(1, nx, one, 0)

    def gather_start(src, dst, k):
        for copy in at_column(src, dst, k):
            copy.start()
        pass_on(src, dst, me, k)

    def gather_pass(src, dst, k):
        for j in list(range(1, ny, 2)) + list(range(2, ny, 2)):
            slot = x * ny + lax.rem(y + j, ny)
            pltpu.make_async_copy(src, src, col_recv.at[k, j]).wait()
            pass_on(dst.at[slot], dst, slot, k)

    def wait_many(dst, tiles, sem):
        some = dst.at[pl.ds(0, tiles)]
        pltpu.make_async_copy(some, some, sem).wait()

    def gather_end(dst, k):
        wait_many(dst, (nx - 1) * ny, all_recv.at[k])

    def gather_sent(src, dst, k):
        for copy in at_column(src, dst, k):
            copy.wait_send()
        wait_many(dst, (nx - 1) * ny, all_send.at[k])

    def halo_copies(k):
        now = field.at[k]
        out = (
            (now.at[0], down.at[k], 1),
            (now.at[rows - 1], up.at[k], 0),
            (now.at[:, 0], right.at[k], 3),
            (now.at[:, cols - 1], left.at[k], 2),
        )
        return [
            pltpu.make_async_remote_copy(
                src_ref=src, dst_ref=dst,
                send_sem=halo_send.at[k, side], recv_sem=halo_recv.at[k, lands],
                device_id=peer, device_id_type=pl.DeviceIdType.MESH,
            )
            for side, ((src, dst, lands), (_, peer)) in enumerate(zip(out, sides))
        ]

    def halo_start(k):
        for (here, _), copy in zip(sides, halo_copies(k)):
            pl.when(here)(copy.start)

    def halo_wait(k, side):
        buf = halos[side].at[k]
        pl.when(sides[side][0])(pltpu.make_async_copy(buf, buf, halo_recv.at[k, side]).wait)

    def near_copies():
        return [
            pltpu.make_async_remote_copy(
                src_ref=nulls, dst_ref=near.at[lands],
                send_sem=near_send.at[side], recv_sem=near_recv.at[lands],
                device_id=peer, device_id_type=pl.DeviceIdType.MESH,
            )
            for side, (lands, (_, peer)) in enumerate(zip((1, 0, 3, 2), sides))
        ]

    loads[0].wait()
    for i in range(rows):
        for j in range(cols):
            p = i * cols + j
            for c in range(0, blk * blk, 128):
                blocks[p, 0, c // 128 : c // 128 + 1] = s_ref[j, i : i + 1, c : c + 128]
            flat = blocks[p, 0, 0 : blk * blk // 128]
            for half in range(128 // blk):
                blocks[p, 1, pl.ds(half, blk * blk // 128, stride=128 // blk), 0:blk] = flat[
                    :, half * blk : (half + 1) * blk
                ]
    for p in range(count):
        hi, lo = cut(relax_weight * blocks[p, 1, :, 0:blk])
        smoother[p] = jnp.concatenate([hi, hi, lo], axis=1)

    def smooth(v):
        return jnp.concatenate(
            [mm(smoother[p], stacked(v[p * blk : (p + 1) * blk])) for p in range(count)], axis=0
        )

    loads[1].wait()
    b = b_ref[...].reshape(size, cases)
    first = smooth(b)
    field[0] = first.reshape(rows, cols, blk, cases)
    for side, (here, _) in enumerate(sides):

        @pl.when(jnp.logical_not(here))
        def _():
            halos[side][...] = jnp.zeros_like(halos[side])
            near[side] = jnp.zeros_like(near[side])

    for load in loads[2:5]:
        load.wait()
    nulls[...] = jnp.zeros_like(nulls)
    for i in range(rows):
        for j in range(cols):
            p = i * cols + j
            for k in range(modes):
                nulls[k : k + 1, p * blk : (p + 1) * blk] = n_ref[
                    j, i : i + 1, k * blk : (k + 1) * blk
                ]
    info[...] = jnp.zeros_like(info)
    info[0:modes, 0 : inv_ref.shape[1]] = inv_ref[...]
    info[modes : modes + 1, :] = jnp.full((1, width), map_ref[0, 0].astype(jnp.float32))

    local[...] = jnp.zeros_like(local)
    loads[5].wait()
    loads[6].wait()
    for i in range(rows):
        for j in range(cols):
            p = i * cols + j
            tiles = [a_ref[i, j, :, s * blk : (s + 1) * blk] for s in range(5)]
            names = [cols_ref[j, i, s] for s in range(5)]
            for d, (di, dj) in enumerate(((0, 0), (-1, 0), (1, 0), (0, -1), (0, 1))):
                e = (i + 1 + di) * (cols + 2) + j + 1 + dj
                tile = tiles[0] * (names[0] == e).astype(jnp.float32)
                for s in range(1, 5):
                    tile = tile + tiles[s] * (names[s] == e).astype(jnp.float32)
                hi, lo = cut(tile)
                ii, jj = i + di, j + dj
                if 0 <= ii < rows and 0 <= jj < cols:
                    q = ii * cols + jj
                    for k, part in enumerate((hi, hi, lo)):
                        at = k * size + q * blk
                        local[p * blk : (p + 1) * blk, at : at + blk] = part
                else:
                    at = (0, j, cols + j, 2 * cols + i, 2 * cols + rows + i)[d]
                    edge[at] = jnp.concatenate([hi, hi, lo], axis=1)

    pl.semaphore_wait(barrier, n - 1)
    halo_start(0)
    for (here, _), copy in zip(sides, near_copies()):
        pl.when(here)(copy.start)
    gather_start(told, told_all, 0)
    info_all[pl.ds(me, 1)] = info[...][None]

    def places():
        for j in range(cols):
            yield 0, j, j, j
        for j in range(cols):
            yield 1, j, cols + j, (rows - 1) * cols + j
        for i in range(rows):
            yield 2, i, 2 * cols + i, i * cols
        for i in range(rows):
            yield 3, i, 2 * cols + rows + i, i * cols + cols - 1

    def operate(v, k):
        inner = mm(local[...], stacked(v))
        parts = [inner[p * blk : (p + 1) * blk] for p in range(count)]
        for side in (2, 3, 0, 1):
            halo_wait(k, side)
            for at_side, at, e, p in places():
                if at_side == side:
                    parts[p] = parts[p] + mm(edge[e], stacked(halos[side][k, at]))
        return jnp.concatenate(parts, axis=0)

    own_n = nulls[...]
    own_hi, own_lo = cut(own_n)
    own_cat = jnp.concatenate([own_hi, own_hi, own_lo], axis=1)

    def restrict(v, k):
        g = mm(own_cat, stacked(v))
        coarse[k] = g
        gather_start(mine(k), theirs_all(k), 1 + k)
        coarse_all[k, pl.ds(me, 1)] = g[None]

    def mine(k):
        return coarse.at[k, 0:modes]

    def theirs_all(k):
        return coarse_all.at[k, :, 0:modes]

    r = b - operate(first, 0)
    restrict(r, 0)
    gather_pass(told, told_all, 0)

    for side, (here, _) in enumerate(sides):
        buf = near.at[side]
        pl.when(here)(pltpu.make_async_copy(buf, buf, near_recv.at[side]).wait)

    def at_rows(t, v):
        pieces = [jnp.zeros_like(v)] * 6
        pieces[t] = v
        return jnp.concatenate(pieces, axis=0)

    def across(v):
        hi, lo = cut(v)
        return jnp.concatenate([hi, lo, hi], axis=1)

    spread = mm_t(local[...], across(at_rows(0, own_n)))
    parts = [spread[p * blk : (p + 1) * blk] for p in range(count)]
    theirs = [near[side] for side in range(4)]
    facing = (
        lambda at: (rows - 1) * cols + at,
        lambda at: at,
        lambda at: at * cols + cols - 1,
        lambda at: at * cols,
    )
    for side, at, e, p in places():
        q = facing[side](at)
        block = theirs[side][:, q * blk : (q + 1) * blk]
        parts[p] = parts[p] + mm_t(edge[e], across(at_rows(1 + side, block)))
    spread = jnp.concatenate(parts, axis=0)
    eye = (
        lax.broadcasted_iota(jnp.int32, (size, size), 0)
        == lax.broadcasted_iota(jnp.int32, (size, size), 1)
    ).astype(jnp.float32).astype(jnp.bfloat16)
    prolong_cut = tuple(
        mm_t(eye, part).astype(jnp.bfloat16) for part in cut(at_rows(0, own_n))
    )

    gather_pass(mine(0), theirs_all(0), 1)
    gather_end(told_all, 0)
    inv_all = info_all[...].reshape(coarse_rows, width)
    ids = [me] + [
        jnp.clip(px, 0, nx - 1) * ny + jnp.clip(py, 0, ny - 1) for _, (px, py) in sides
    ]
    lane = lax.broadcasted_iota(jnp.int32, (8, coarse_rows), 1)
    row = lax.broadcasted_iota(jnp.int32, (8, coarse_rows), 0)
    pick = []
    for d in ids:
        tile = info_all[pl.ds(d, 1)].reshape(8, width)
        label = jnp.broadcast_to(tile[modes : modes + 1, 0:1], (8, coarse_rows))
        wanted = label * 8.0 + row.astype(jnp.float32)
        hit = jnp.where(lane.astype(jnp.float32) == wanted, 1.0, 0.0)
        pick.append(jnp.where(row < modes, hit, 0.0))
    pick.append(jnp.zeros((8, coarse_rows), jnp.float32))
    picked = lax.dot_general(
        jnp.concatenate(pick, axis=0), inv_all, (((1,), (0,)), ((), ())),
        precision=highest, preferred_element_type=jnp.float32,
    )
    lane3 = lax.broadcasted_iota(jnp.int32, (n, 8, width), 2).astype(jnp.float32)
    row3 = lax.broadcasted_iota(jnp.int32, (n, 8, width), 1)
    labels = jnp.broadcast_to(info_all[...][:, modes : modes + 1, :], (n, 8, width))
    order = jnp.where(lane3 == labels * float(modes) + row3.astype(jnp.float32), 1.0, 0.0)
    order = jnp.where(row3 < modes, order, 0.0).reshape(coarse_rows, width)
    solve = mm_t(picked, order, precision=highest)
    solve_cut = cut(solve)
    spread_cut = cut(mm3(cut(spread), solve))

    def correct(k):
        gather_end(theirs_all(k), 1 + k)
        g = coarse_all[k].reshape(coarse_rows, cases)
        return mm3(prolong_cut, mm3(solve_cut, g)), mm3(spread_cut, g)

    def relax(v, k):
        s = smooth(v)
        field[k] = s.reshape(rows, cols, blk, cases)
        halo_start(k)
        return s, v - operate(s, k)

    up_by, down_by = correct(0)
    precond = first + up_by
    r = r - down_by
    s, r = relax(r, 1)
    precond = precond + s
    s, r = relax(r, 2)
    precond = precond + s
    restrict(r, 1)
    gather_pass(mine(1), theirs_all(1), 2)
    up_by, down_by = correct(1)
    precond = precond + up_by
    r = r - down_by
    s, r = relax(r, 3)
    precond = precond + s

    image = b - r
    sums[...] = jnp.concatenate(
        [
            jnp.sum(b * precond, axis=0, keepdims=True),
            jnp.sum(precond * image, axis=0, keepdims=True),
            jnp.zeros((6, cases), jnp.float32),
        ],
        axis=0,
    )

    def share(j, carry):
        peer = lax.rem(me + j, n)
        pltpu.make_async_remote_copy(
            src_ref=sums.at[0:2], dst_ref=sums_all.at[me, 0:2], send_sem=sum_send, recv_sem=sum_recv,
            device_id=(peer // ny, lax.rem(peer, ny)), device_id_type=pl.DeviceIdType.MESH,
        ).start()
        return carry

    lax.fori_loop(1, n, share, 0)
    sums_all[pl.ds(me, 1)] = sums[...][None]
    precond_ref[...] = precond.reshape(rows, cols, blk, cases)
    image_ref[...] = image.reshape(rows, cols, blk, cases)
    pairs = sums_all.at[:, 0:2]
    wait_many(pairs, n - 1, sum_recv)
    total = jnp.sum(sums_all[:, 0:2], axis=0)
    alpha_ref[...] = total[0:1] / total[1:2]

    for k in range(4):
        for (here, _), copy in zip(sides, halo_copies(k)):
            pl.when(here)(copy.wait_send)
    for (here, _), copy in zip(sides, near_copies()):
        pl.when(here)(copy.wait_send)
    gather_sent(told, told_all, 0)
    gather_sent(mine(0), theirs_all(0), 1)
    gather_sent(mine(1), theirs_all(1), 2)
    wait_many(pairs, n - 1, sum_send)


def finish_kernel(b_ref, p_ref, i_ref, alpha_ref, sol_ref, res_ref, held, scale, sems, scale_sem):
    rows = b_ref.shape[0]
    first = pltpu.make_async_copy(alpha_ref, scale, scale_sem)
    first.start()

    def move(k, i):
        ref = (p_ref, i_ref, b_ref, sol_ref, res_ref)[k]
        ends = (ref.at[i], held.at[k, i])
        return pltpu.make_async_copy(*(ends if k < 3 else ends[::-1]), sems.at[k, i])

    for i in range(rows):
        for k in range(3):
            move(k, i).start()
    first.wait()
    alpha = scale[...].reshape(1, 1, -1)
    for i in range(rows):
        move(0, i).wait()
        held[3, i] = alpha * held[0, i]
        move(3, i).start()
        move(1, i).wait()
        move(2, i).wait()
        held[4, i] = held[2, i] - alpha * held[1, i]
        move(4, i).start()
    for i in range(rows):
        move(3, i).wait()
        move(4, i).wait()


def fused(
    nx, ny,
    load_cases, matrix_tiles, block_cols, smoother_blocks, near_null, coarse_map, coarse_inverse
):
    rows, cols, blk, cases = load_cases.shape
    count = rows * cols
    modes = near_null.shape[2] // blk
    n = nx * ny
    width = -(-coarse_inverse.shape[1] // 128) * 128
    block_cols = jnp.transpose(block_cols, (1, 0, 2))
    smoother_blocks = jnp.transpose(smoother_blocks, (1, 0, 2))
    near_null = jnp.transpose(near_null, (1, 0, 2))
    vmem = pl.BlockSpec(memory_space=pltpu.VMEM)
    hbm = pl.BlockSpec(memory_space=pltpu.HBM)
    f32, bf16 = jnp.float32, jnp.bfloat16
    shape = jax.ShapeDtypeStruct(load_cases.shape, f32)
    precond, image, alpha = pl.pallas_call(
        functools.partial(step_kernel, nx, ny, modes),
        out_shape=(shape, shape, jax.ShapeDtypeStruct((1, cases), f32)),
        in_specs=[hbm] * 7,
        out_specs=(vmem, vmem, vmem),
        scratch_shapes=[
            pltpu.VMEM(load_cases.shape, f32),
            pltpu.VMEM(matrix_tiles.shape, f32),
            pltpu.SMEM(block_cols.shape, jnp.int32),
            pltpu.VMEM(smoother_blocks.shape, f32),
            pltpu.VMEM(near_null.shape, f32),
            pltpu.SMEM(coarse_map.shape, jnp.int32),
            pltpu.VMEM(coarse_inverse.shape, f32),
            pltpu.SemaphoreType.DMA((7,)),
            pltpu.VMEM((count, 2, blk, 128), f32),
            pltpu.VMEM((8, count * blk), f32),
            pltpu.VMEM((4, rows, cols, blk, cases), f32),
            pltpu.VMEM((4, cols, blk, cases), f32),
            pltpu.VMEM((4, cols, blk, cases), f32),
            pltpu.VMEM((4, rows, blk, cases), f32),
            pltpu.VMEM((4, rows, blk, cases), f32),
            pltpu.VMEM((count * blk, 3 * count * blk), bf16),
            pltpu.VMEM((2 * (rows + cols), blk, 3 * blk), bf16),
            pltpu.VMEM((count, blk, 3 * blk), bf16),
            pltpu.VMEM((8, width), f32),
            pltpu.VMEM((n, 8, width), f32),
            pltpu.VMEM((4, 8, count * blk), f32),
            pltpu.VMEM((2, 8, cases), f32),
            pltpu.VMEM((2, n, 8, cases), f32),
            pltpu.VMEM((8, cases), f32),
            pltpu.VMEM((n, 8, cases), f32),
            pltpu.SemaphoreType.DMA((4, 4)),
            pltpu.SemaphoreType.DMA((4, 4)),
            pltpu.SemaphoreType.DMA((4,)),
            pltpu.SemaphoreType.DMA((4,)),
            pltpu.SemaphoreType.DMA((3, ny)),
            pltpu.SemaphoreType.DMA((3, ny)),
            pltpu.SemaphoreType.DMA((3,)),
            pltpu.SemaphoreType.DMA((3,)),
            pltpu.SemaphoreType.DMA,
            pltpu.SemaphoreType.DMA,
        ],
        compiler_params=pltpu.CompilerParams(
            collective_id=0, has_side_effects=True, vmem_limit_bytes=60 * 2**20
        ),
    )(
        load_cases, matrix_tiles, block_cols, smoother_blocks, near_null, coarse_map,
        coarse_inverse,
    )
    return pl.pallas_call(
        finish_kernel,
        out_shape=(shape, shape),
        in_specs=[hbm, hbm, hbm, hbm],
        out_specs=(hbm, hbm),
        scratch_shapes=[
            pltpu.VMEM((5,) + load_cases.shape, f32),
            pltpu.VMEM((1, cases), f32),
            pltpu.SemaphoreType.DMA((5, rows)),
            pltpu.SemaphoreType.DMA,
        ],
        compiler_params=pltpu.CompilerParams(vmem_limit_bytes=60 * 2**20),
    )(load_cases, precond, image, alpha)


def per_device(
    load_cases, matrix_tiles, block_cols, smoother_blocks, near_null, coarse_map, coarse_inverse
):
    agg_rows, agg_cols, block_size, case_count = load_cases.shape
    mode_count = near_null.shape[2] // block_size
    coarse_total = coarse_inverse.shape[1]
    coarse_aggs = coarse_total // mode_count
    modes = near_null.reshape(agg_rows, agg_cols, mode_count, block_size)
    inverse_blocks = smoother_blocks.reshape(agg_rows, agg_cols, block_size, block_size)

    def operate(vector_field):
        extended = padded(vector_field, (("gx", 0), ("gy", 1)), 1)
        flattened = extended.reshape(-1, block_size, case_count)
        picked = flattened[block_cols].reshape(agg_rows, agg_cols, -1, case_count)
        return jnp.einsum("ijbk,ijkr->ijbr", matrix_tiles, picked, precision=highest)

    def smooth(defect):
        return relax_weight * jnp.einsum(
            "ijab,ijbr->ijar", inverse_blocks, defect, precision=highest
        )

    def correct(defect):
        contrib = jnp.einsum("ijkb,ijbr->ijkr", modes, defect, precision=highest)
        own_part = jnp.sum(contrib, axis=(0, 1))
        my_label = coarse_map[0, 0]
        label_value = jnp.reshape(my_label.astype(jnp.float32), (1,))
        pieces, labels = (
            lax.all_gather(own_part[None], ("gx", "gy"), axis=0, tiled=True),
            lax.all_gather(label_value, ("gx", "gy"), axis=0, tiled=True),
        )
        label_ids = labels.astype(jnp.int32)
        placing = (label_ids[:, None] == jnp.arange(coarse_aggs, dtype=jnp.int32)[None, :]).astype(
            jnp.float32
        )
        ordered = jnp.einsum("dc,dkr->ckr", placing, pieces, precision=highest).reshape(
            coarse_total, case_count
        )
        own_rows = jnp.dot(coarse_inverse, ordered, precision=highest)
        solved = lax.all_gather(own_rows, ("gx", "gy"), axis=0, tiled=True)
        mine = lax.dynamic_slice_in_dim(solved, my_label * mode_count, mode_count, 0)
        coarse_back = jnp.broadcast_to(
            mine[None, None], (agg_rows, agg_cols, mode_count, case_count)
        )
        return jnp.einsum("ijkb,ijkr->ijbr", modes, coarse_back, precision=highest)

    first = smooth(load_cases)
    first = first + correct(load_cases - operate(first))
    precond = first + smooth(load_cases - operate(first))
    defect = load_cases - operate(precond)
    update = smooth(defect)
    update = update + correct(defect - operate(update))
    update = update + smooth(defect - operate(update))
    precond = precond + update
    local_aligned = jnp.sum(load_cases * precond, axis=(0, 1, 2))
    aligned = lax.psum(local_aligned, ("gx", "gy"))
    image = operate(precond)
    curved = lax.psum(jnp.sum(precond * image, axis=(0, 1, 2)), ("gx", "gy"))
    alpha = aligned / curved
    solution = alpha * precond
    residual = load_cases - alpha * image
    return (solution, residual)


def solution(mesh):
    nx, ny = mesh.shape["gx"], mesh.shape["gy"]
    step = functools.partial(fused, nx, ny) if nx * ny <= 128 else per_device
    placed = (
        P("gx", "gy", None, None),
        P("gx", "gy", None, None),
        P("gx", "gy", None),
        P("gx", "gy", None),
        P("gx", "gy", None),
        P("gx", "gy"),
        P(("gx", "gy"), None),
    )
    return jax.shard_map(
        step,
        mesh=mesh,
        in_specs=placed,
        out_specs=(P("gx", "gy", None, None), P("gx", "gy", None, None)),
        check_vma=False,
    )
```
